32 devices in a mesh: leaf: 4 (over z), front: 8 (over y, x, core).
Axes of the slice: x: 2, y: 2, z: 4, core: 2. Of those that a mesh axis runs over, the one named last changes fastest.
Arguments:
- rhs_leaf: float32 [4, 2048, 64], P('leaf', 'front'), may hold values from -2.4 to 2.4
- diag_inv: bfloat16 [4, 8, 256, 256], P('leaf', 'front'), as said below
- sub_block: bfloat16 [4, 8, 256, 256], P('leaf', 'front'), as said below
- coupling: bfloat16 [4, 256, 2048], P('leaf', None, 'front'), may hold values from -0.25 to 0.25
- update_rows: int32 [4, 256], P('leaf'), may hold values from 0 to 1023, as said below
- rhs_sep: float32 [1024, 64], P('leaf'), may hold values from -6 to 6
- sep_inv: bfloat16 [1024, 1024], P('front', 'leaf'), as said below
Outputs:
- leaf_solution: float32 [4, 2048, 64], P('leaf', 'front')
- separator_solution: float32 [1024, 64], P('leaf')
The draws below stay inside these ranges and needn't reach their ends.
Inputs may be any that keep to these rules, and one draw needn't show every extreme that they name: `update_rows`: within a group the 256 indices are distinct and increasing, and include the first and the last separator row. `diag_inv`: each 256 x 256 block is lower triangular. `sub_block`: each 256 x 256 block is lower triangular. `sep_inv`: lower triangular.
All inputs are finite; a program needn't handle non-finite values.
Results may differ from the reference program's by a relative error of at most 0.0003.
Values may be sent and summed in bfloat16 or wider, within the bound.
A program may use at most 64 MiB of HBM per device.

```python
import math
import jax
import jax.numpy as jnp
from jax import lax

W = 256
R = 64
U = 256
S = 1024
SUBTREE_GROUPS = 4
CHAIN_SUPERNODES = 8
ROWS = 2048


def factor_parts(key):
    folded = jax.random.fold_in(key, 11)
    parallel_lanes = jax.random.split(folded, 8)
    slow_share = 0.5
    is_slow = jax.random.bernoulli(parallel_lanes[0], slow_share, (SUBTREE_GROUPS, 1, W))
    survive = jax.random.uniform(parallel_lanes[1], (SUBTREE_GROUPS, 1, 1), minval=0.15, maxval=0.3)
    per_step = jnp.exp(jnp.log(survive / 0.36) / CHAIN_SUPERNODES)
    jitter = jax.random.uniform(parallel_lanes[2], (SUBTREE_GROUPS, CHAIN_SUPERNODES, 1), minval=0.5, maxval=1.5)
    slow_rate = per_step ** jitter
    spread_begin = jax.random.randint(parallel_lanes[3], (SUBTREE_GROUPS, 2), 0, CHAIN_SUPERNODES)
    current_place = jnp.arange(CHAIN_SUPERNODES)
    spreading_active = jnp.any(current_place[None, :, None] == spread_begin[:, None, :], axis=2)[:, :, None]
    slow_rate = jnp.where(spreading_active, 0.6 * slow_rate, slow_rate)
    fast_rate = jax.random.uniform(parallel_lanes[4], (SUBTREE_GROUPS, CHAIN_SUPERNODES, W), minval=0.2, maxval=0.6)
    decay_rate = jnp.where(is_slow, slow_rate, fast_rate)
    pivots = jnp.exp(jax.random.uniform(parallel_lanes[5], (SUBTREE_GROUPS, CHAIN_SUPERNODES, W), minval=math.log(0.7), maxval=math.log(1.4)))
    identity_w = jnp.eye(W, dtype=jnp.float32)
    lower_first = jnp.tril(jax.random.normal(parallel_lanes[6], (SUBTREE_GROUPS, CHAIN_SUPERNODES, W, W)) * (0.3 / math.sqrt(W)), -1)
    lower_second = jnp.tril(jax.random.normal(parallel_lanes[7], (SUBTREE_GROUPS, CHAIN_SUPERNODES, W, W)) * (0.3 / math.sqrt(W)), -1)
    inverse_part = lower_first + pivots[..., None] * identity_w
    couple_part = lower_second + (-decay_rate / pivots)[..., None] * identity_w
    return (inverse_part, couple_part)


def draw_diag_inv(key, part):
    inverse_part, couple_part = factor_parts(key)
    return inverse_part.astype(jnp.bfloat16)


def draw_sub_block(key, part):
    inverse_part, couple_part = factor_parts(key)
    return couple_part.astype(jnp.bfloat16)


def draw_update_rows(key, part):
    parallel_lanes = jax.random.split(jax.random.fold_in(key, 5), SUBTREE_GROUPS)
    middle = jax.vmap(lambda stream: jax.random.permutation(stream, S - 2))(parallel_lanes)[:, :U - 2] + 1
    leading_row = jnp.zeros((SUBTREE_GROUPS, 1), jnp.int32)
    last_row = jnp.full((SUBTREE_GROUPS, 1), S - 1, jnp.int32)
    chosen = jnp.concatenate([leading_row, middle.astype(jnp.int32), last_row], axis=1)
    return jnp.sort(chosen, axis=1).astype(jnp.int32)


def draw_sep_inv(key, part):
    parallel_lanes = jax.random.split(jax.random.fold_in(key, 23), 2)
    random_part = jax.random.normal(parallel_lanes[0], (S, S))
    lower_part = jnp.tril(random_part * (0.5 / math.sqrt(S)), -1)
    diagonal = jnp.exp(jax.random.uniform(parallel_lanes[1], (S,), minval=math.log(0.5), maxval=math.log(2.0)))
    return (lower_part + diagonal[:, None] * jnp.eye(S, dtype=jnp.float32)).astype(jnp.bfloat16)


def level_of(key, extent, shards, least, largest):
    gain = 1.0
    for axis_at, blocks in shards:
        heights = jax.random.uniform(jax.random.fold_in(jax.random.fold_in(key, 6), axis_at), (blocks,), jnp.float32, least / len(shards), largest / len(shards))
        gain = gain * jnp.repeat(jnp.exp(heights), extent[axis_at] // blocks).reshape((-1,) + (1,) * (len(extent) - 1 - axis_at))
    return gain


def normal_values(key, dims, scale, most, pieces=(), held_as=jnp.bfloat16):
    level = level_of(key, dims, pieces, -0.22, 0.18) if pieces else 1.0
    array = jax.random.normal(key, dims, jnp.float32) * scale * level
    return jnp.minimum(jnp.maximum(array, -most), most).astype(held_as)


def setup_inputs(seed: int = 0) -> dict:
    arg_keys = jax.random.split(jax.random.key(seed), 8)
    rhs_leaf = normal_values(arg_keys[0], (SUBTREE_GROUPS, ROWS, R), 0.3, 2.4, ((0, 4), (1, 8)), jnp.float32)
    diag_inv = draw_diag_inv(jax.random.fold_in(arg_keys[7], 71), 0)
    sub_block = draw_sub_block(jax.random.fold_in(arg_keys[7], 71), 0)
    coupling = normal_values(arg_keys[3], (SUBTREE_GROUPS, U, ROWS), (ROWS // 4) ** -0.5, 0.25, ((0, 4), (2, 8)))
    update_rows = draw_update_rows(jax.random.fold_in(arg_keys[7], 71), 0)
    rhs_sep = normal_values(arg_keys[5], (S, R), 1.0, 6.0, ((0, 4),), jnp.float32)
    sep_inv = draw_sep_inv(jax.random.fold_in(arg_keys[7], 71), 0)
    return {"rhs_leaf": rhs_leaf, "diag_inv": diag_inv, "sub_block": sub_block, "coupling": coupling, "update_rows": update_rows, "rhs_sep": rhs_sep, "sep_inv": sep_inv}


PRECISE = lax.Precision.HIGHEST


def product(left, right):
    return jnp.matmul(left, right, precision=PRECISE)


def reference(rhs_leaf, diag_inv, sub_block, coupling, update_rows, rhs_sep, sep_inv):
    blocks = rhs_leaf.reshape(SUBTREE_GROUPS, CHAIN_SUPERNODES, W, R)

    def forward_group(inputs):
        inverses, couples, rights = inputs

        def advance(previous, item):
            inverse, couple, right = item
            value = product(inverse.astype(jnp.float32), right - product(couple.astype(jnp.float32), previous))
            return value, value

        _, values = lax.scan(advance, jnp.zeros((W, R), jnp.float32), (inverses, couples, rights))
        return values.reshape(ROWS, R)

    forward_y = lax.map(forward_group, (diag_inv, sub_block, blocks))

    def group_update(inputs):
        block_rows, values = inputs
        return product(block_rows.astype(jnp.float32), values)

    updates = lax.map(group_update, (coupling, forward_y))
    update_total = jnp.zeros((S, R), jnp.float32).at[update_rows.reshape(-1)].add(updates.reshape(SUBTREE_GROUPS * U, R))
    inverse_sep = sep_inv.astype(jnp.float32)
    sep_forward = product(inverse_sep, rhs_sep - update_total)
    separator_solution = product(inverse_sep.T, sep_forward)

    def backward_group(inputs):
        inverses, couples, values, block_rows, indices = inputs
        selected_entries = separator_solution[indices]
        adjusted = values - product(block_rows.astype(jnp.float32).T, selected_entries)
        following = jnp.concatenate([couples[1:], jnp.zeros((1, W, W), couples.dtype)], axis=0)

        def retreat(later, item):
            inverse, couple, right = item
            value = product(inverse.astype(jnp.float32).T, right - product(couple.astype(jnp.float32).T, later))
            return value, value

        _, solved = lax.scan(retreat, jnp.zeros((W, R), jnp.float32), (inverses, following, adjusted.reshape(CHAIN_SUPERNODES, W, R)), reverse=True)
        return solved.reshape(ROWS, R)

    leaf_solution = lax.map(backward_group, (diag_inv, sub_block, forward_y, coupling, update_rows))
    return leaf_solution, separator_solution
```

```python
import functools
import types

import jax
import jax.numpy as jnp
from jax import lax
from jax.experimental import pallas as pl
from jax.experimental.pallas import tpu as pltpu
from jax.sharding import PartitionSpec as P

MESH = pl.DeviceIdType.MESH
F32 = jnp.float32
BF16 = jnp.bfloat16


def halves(x):
    head = x.astype(BF16)
    rest = (x - head.astype(F32)).astype(BF16)
    return jnp.concatenate([head, rest], axis=0)


def joined(both):
    rows = both.shape[0] // 2
    return both[:rows] + both[rows:]


def dot(a, b):
    return jnp.dot(a, b, preferred_element_type=F32)


def dot_t(a, b):
    return lax.dot_general(a, b, (((1,), (1,)), ((), ())), preferred_element_type=F32)


def times(x, w):
    return joined(dot(halves(x), w))


def times_t(x, w):
    return joined(dot_t(halves(x), w))


def split(x):
    head = x.astype(BF16)
    return head, (x - head.astype(F32)).astype(BF16)


def through(x, w, multiply):
    head, rest = w
    both = halves(x)
    return joined(multiply(both, head)) + multiply(both[: x.shape[0]], rest)


def composed(a, b):
    return dot(a[0], b[0]) + (dot(a[1], b[0]) + dot(a[0], b[1]))


def kernel(groups, chips, skips, chunk, names, r_ref, d_ref, b_ref, c_ref, idx_ref, rs_ref, sp_ref, out_ref, sol_ref, *refs):
    v = types.SimpleNamespace(**dict(zip(names, refs)))
    plane = lax.axis_index("leaf")
    front = lax.axis_index("front")
    chip = front // 2
    core = front % 2
    other = 1 - core
    last = chips - 1
    root = chips - 2
    is_root = chip == root
    is_last = chip == last
    is_mid = jnp.logical_and(chip > 0, chip < root)
    sibling = (plane, chip * 2 + other)
    half = v.yin.shape[0]
    picks = v.uin.shape[1]
    deep, wide = v.sep.shape[3:]
    fac = v.fac

    def remote(src, dst, send, recv, to):
        return pltpu.make_async_remote_copy(
            src_ref=src, dst_ref=dst, send_sem=send, recv_sem=recv, device_id=to, device_id_type=MESH
        )

    def near(c):
        return (plane, c * 2 + core)

    mine_rows = pl.ds(pl.multiple_of(core * half, half), half)
    other_rows = pl.ds(pl.multiple_of(other * half, half), half)

    barrier = pltpu.get_barrier_semaphore()

    def signal(sem, to):
        pl.semaphore_signal(sem, inc=1, device_id=to, device_id_type=MESH)

    signal(barrier, sibling)
    for c in range(chips):
        @pl.when(chip != c)
        def _(c=c):
            signal(barrier, near(c))
    for g in range(1, groups):
        @pl.when(plane < g)
        def _(g=g):
            @pl.when(is_root)
            def _():
                for c in range(chips):
                    signal(barrier, (g, c * 2 + core))

            @pl.when(jnp.logical_not(is_root))
            def _():
                signal(barrier, (g, root * 2 + core))

    loads = [pltpu.make_async_copy(r_ref, v.rown, v.loc_s.at[0])]
    for i, ref in enumerate((d_ref, b_ref, c_ref)):
        loads.append(pltpu.make_async_copy(ref, fac.at[i, core], v.loc_s.at[i + 1]))
    for copy in loads:
        copy.start()
    for copy in loads:
        copy.wait()

    pl.semaphore_wait(barrier, chips + jnp.where(is_root, plane * chips, plane))

    swaps = [remote(v.rown.at[other_rows], v.rin, v.swap_s.at[0], v.swap_r.at[0], sibling)]
    for i in range(3):
        part = fac.at[i, core]
        swaps.append(remote(part, part, v.swap_s.at[i + 1], v.swap_r.at[i + 1], sibling))
    for copy in swaps:
        copy.start()

    @pl.when(is_root)
    def _():
        for g in range(groups - 1):
            @pl.when(plane > g)
            def _(g=g):
                for c in range(chips):
                    signal(v.up, (g, c * 2 + core))

    for copy in swaps[:3]:
        copy.wait_recv()
    mine = v.rown[mine_rows]
    theirs = v.rin[...]
    r_first = jnp.where(core == 0, mine, theirs)
    r_second = jnp.where(core == 0, theirs, mine)

    y_copy = remote(v.yout, v.yin, v.y_s, v.y_r, near(jnp.minimum(chip + 1, last)))
    u_copy = remote(v.uout, v.uin, v.u_s, v.u_r, near(jnp.minimum(chip + 1, root)))
    ul_copy = remote(v.uout, v.ulast, v.u_s, v.ul_r, near(root))
    s_copy = remote(v.maps.at[core, 1], v.slast.at[core], v.s_s, v.s_r, near(root))
    s_onward = remote(v.slast.at[core], v.slast.at[core], v.sf_s, v.sf_r, sibling)
    s_theirs = remote(v.slast.at[other], v.slast.at[other], v.sf_s, v.sf_r, sibling)
    u_copies = []
    for step in range(1, groups):
        g = lax.rem(plane + step, groups)
        u_copies.append(
            remote(v.uout, v.ubuf.at[plane], v.ux_s.at[step - 1], v.ux_r.at[plane], (g, root * 2 + core))
        )

    own_first = times_t(r_first, fac[0, 0])
    own_second = times_t(r_second - times_t(own_first, fac[1, 1]), fac[0, 1])

    @pl.when(chip == 0)
    def _():
        v.yin[...] = jnp.zeros_like(v.yin)
        v.yout[...] = own_second
        y_copy.start()

    swaps[3].wait_recv()
    own_update = times_t(own_first, fac[2, 0]) + times_t(own_second, fac[2, 1])

    @pl.when(jnp.logical_or(chip == 0, is_last))
    def _():
        v.uout[...] = own_update

    @pl.when(chip == 0)
    def _():
        u_copy.start()

    @pl.when(is_last)
    def _():
        ul_copy.start()

    early = split(dot(fac[0, 0], fac[1, 0]))
    late = split(dot(fac[0, 1], fac[1, 1]))
    whole = split(composed(late, early))
    seen = split(
        dot(fac[2, 1], whole[0]) - dot(fac[2, 0], early[0])
        + (dot(fac[2, 1], whole[1]) - dot(fac[2, 0], early[1]))
    )
    for part in range(2):
        v.maps[part, 0] = whole[part]
        v.maps[part, 1] = seen[part]

    @pl.when(is_last)
    def _():
        s_copy.start()

    @pl.when(plane < groups - 1)
    def _():
        pl.semaphore_wait(v.up, groups - 1 - plane)

    def sep_copy(g):
        return remote(sp_ref, v.sep.at[plane, core, chip], v.sep_s.at[g], v.sep_r.at[plane], (g, root * 2 + core))

    useful = chip >= (plane * wide) // (2 * deep)

    def sep_sends(action):
        for g in range(groups):
            here = jnp.logical_and(is_root, plane == g)

            @pl.when(jnp.logical_and(useful, jnp.logical_not(here)))
            def _(g=g):
                action(sep_copy(g))

    sep_sends(lambda copy: copy.start())

    def peers(action):
        for g in range(groups):
            @pl.when(plane != g)
            def _(g=g):
                action(g, (g, root * 2 + core))

    def rs_copy(g, to, at):
        return remote(rs_ref.at[mine_rows], v.rsbuf.at[at], v.rs_s.at[g], v.rs_r.at[at], to)

    def id_copy(g, to, at):
        return remote(idx_ref, v.idx.at[at], v.id_s.at[g], v.id_r.at[at], to)

    def sep_part(g, k):
        return v.sep.at[g, k, pl.ds(skips[g], chips - skips[g])]

    @pl.when(is_root)
    def _():
        for g in range(groups):
            if skips[g] <= root:
                @pl.when(plane == g)
                def _(g=g):
                    pltpu.make_async_copy(sp_ref, v.sep.at[g, core, root], v.sep_r.at[g]).start()

        own_rs = pltpu.make_async_copy(rs_ref.at[mine_rows], v.rsbuf.at[plane], v.loc_s.at[4])
        own_id = pltpu.make_async_copy(idx_ref, v.idx.at[plane], v.loc_s.at[5])
        own_rs.start()
        own_id.start()
        peers(lambda g, to: id_copy(g, to, plane).start())
        peers(lambda g, to: rs_copy(g, to, plane).start())
        for g in range(groups):
            for c in range(skips[g]):
                v.sep[g, :, c] = jnp.zeros((2, deep, wide), BF16)
        own_id.wait()
        own_rs.wait()
        peers(lambda g, to: id_copy(g, to, g).wait_recv())
        lanes = min(128, picks)
        for g in range(groups):
            index = jnp.transpose(jnp.broadcast_to(v.idx[g].astype(F32), (lanes, picks)))
            for at in range(0, groups * wide, lanes):
                column = lax.broadcasted_iota(jnp.int32, (picks, lanes), 1) + at
                v.sel[g * picks : (g + 1) * picks, at : at + lanes] = (
                    (index == column.astype(F32)).astype(F32).astype(BF16)
                )
        s_copy.wait_recv()
        s_onward.start()
        s_theirs.wait_recv()
        total = split(seen[0].astype(F32) + seen[1].astype(F32) + composed((v.slast[0], v.slast[1]), whole))
        v.maps[0, 1] = total[0]
        v.maps[1, 1] = total[1]
        ul_copy.wait_recv()
        v.upre[...] = v.ulast[...] + own_update + through(own_second, (v.slast[0], v.slast[1]), dot_t)

    @pl.when(is_mid)
    def _():
        v.upre[...] = own_update

    @pl.when(chip > 0)
    def _():
        y_copy.wait_recv()

    heard = v.yin[...]
    second = own_second + through(heard, whole, dot_t)

    @pl.when(jnp.logical_and(chip > 0, jnp.logical_not(is_last)))
    def _():
        v.yout[...] = second
        y_copy.start()
        update = v.upre[...] + through(heard, (v.maps[0, 1], v.maps[1, 1]), dot_t)
        u_copy.wait_recv()
        v.uout[...] = update + v.uin[...]

        @pl.when(is_root)
        def _():
            for copy in u_copies:
                copy.start()

        @pl.when(jnp.logical_not(is_root))
        def _():
            u_copy.start()

    def map_copy(c, to):
        return remote(v.maps.at[core], v.later.at[c - 1, core], v.m_s.at[to], v.m_r.at[c - 1], near(to))

    def map_onward(c, k):
        part = v.later.at[c - 1, k]
        return remote(part, part, v.mf_s.at[c - 1], v.mf_r.at[c - 1], sibling)

    def turned_copy(c, to):
        return remote(v.tout, v.tbuf.at[c - 1], v.t_s.at[to], v.t_r.at[c - 1], near(to))

    def to_earlier(limit, action):
        for c in range(1, limit):
            @pl.when(chip == c)
            def _(c=c):
                for to in reversed(range(c)):
                    action(c, to)

    def from_later(limit, action):
        for c in reversed(range(1, limit)):
            @pl.when(chip < c)
            def _(c=c):
                action(c)

    to_earlier(last, lambda c, to: map_copy(c, to).start())
    first = own_first - times_t(times_t(heard, fac[1, 0]), fac[0, 0])
    v.tout[...] = times(times(first, fac[0, 0]), fac[1, 0]) - through(second, whole, dot)
    to_earlier(chips, lambda c, to: turned_copy(c, to).start())

    def block(g, c):
        return jnp.concatenate([v.sep[g, 0, c], v.sep[g, 1, c]], axis=0)

    own_rows = pl.ds(pl.multiple_of(plane * picks, picks), picks)

    @pl.when(is_root)
    def _():
        for g in range(groups):
            part = sep_part(g, core)
            pltpu.make_async_copy(part, part, v.sep_r.at[g]).wait()
            remote(part, part, v.fwd_s.at[g], v.fwd_r.at[g], sibling).start()
        peers(lambda g, to: rs_copy(g, to, g).wait_recv())
        for g in range(groups):
            part = sep_part(g, other)
            remote(part, part, v.fwd_s.at[g], v.fwd_r.at[g], sibling).wait_recv()

        def gather(step, carry):
            rows = pl.ds(pl.multiple_of(step * chunk, chunk), chunk)
            for c in range(chips):
                taken = 0
                for g in range(groups):
                    if skips[g] <= c:
                        taken = taken + dot_t(v.sel[rows, g * wide : (g + 1) * wide], block(g, c))
                v.at[c, rows] = taken.astype(BF16)
            return carry

        lax.fori_loop(0, groups * picks // chunk, gather, 0, unroll=groups * picks == chunk)

        def pair(step, carry):
            rows = pl.ds(pl.multiple_of(step * chunk, chunk), chunk)
            near_part, far_part = 0, 0
            for c in range(chips):
                near_part = near_part + dot_t(v.at[c, rows], v.at[c, own_rows])
                far_part = far_part + dot(v.at[c, rows], block(plane, c))
            for part, value in enumerate(split(near_part)):
                v.gz[part, rows] = value
            for part, value in enumerate(split(far_part)):
                v.gs[part, rows] = value
            return carry

        lax.fori_loop(0, groups * picks // chunk, pair, 0, unroll=groups * picks == chunk)

        found, solved = 0, 0
        for c in range(chips):
            ahead = 0
            for g in range(groups):
                if skips[g] <= c:
                    ahead = ahead + times_t(v.rsbuf[g], block(g, c))
            found = found + times_t(ahead, v.at[c, own_rows])
            solved = solved + times(ahead, block(plane, c))
        update = v.uout[...]
        v.zpre[...] = found - through(update, (v.gz[0, own_rows], v.gz[1, own_rows]), dot)
        v.spre[...] = solved - through(update, (v.gs[0, own_rows], v.gs[1, own_rows]), dot)
        for part in range(2):
            v.tn[part] = v.slast[part]

    @pl.when(is_last)
    def _():
        v.tn[...] = jnp.zeros_like(v.tn)

    def pass_on(c):
        map_copy(c, 0).wait_recv()
        map_onward(c, core).start()

    from_later(last, pass_on)

    def step_map(c):
        map_onward(c, other).wait_recv()
        got = v.later.at[c - 1]
        if c == root:
            for part in range(2):
                v.tn[part] = got[part, 1]
        else:
            value = got[0, 1].astype(F32) + got[1, 1].astype(F32) + composed((v.tn[0], v.tn[1]), (got[0, 0], got[1, 0]))
            for part, value in enumerate(split(value)):
                v.tn[part] = value

    from_later(last, step_map)

    back = split(dot(fac[2, 1], fac[0, 1]) + dot(v.tn[0], fac[0, 1]) + dot(v.tn[1], fac[0, 1]))
    between = split(dot(back[0], fac[1, 1]) + dot(back[1], fac[1, 1]))
    front_map = split(dot(fac[2, 0], fac[0, 0]) - (dot(between[0], fac[0, 0]) + dot(between[1], fac[0, 0])))
    for part in range(2):
        v.fmap[0, part] = front_map[part]
        v.fmap[1, part] = back[part]

    targets = [near(c) for c in reversed(range(root))] + [near(last)]
    across = [(plane, c * 2 + other) for c in reversed(range(root))] + [(plane, last * 2 + other)]
    order = [to for pair_ in zip(targets, across) for to in pair_] + [sibling]
    z_copies = [remote(v.zbuf.at[core], v.zbuf.at[core], v.z_s.at[i], v.z_r.at[core], to) for i, to in enumerate(order)]
    so_copies = [remote(v.sol.at[core], v.sol.at[core], v.so_s.at[i], v.so_r.at[core], to) for i, to in enumerate(order)]

    @pl.when(is_root)
    def _():
        found, solved = v.zpre[...], v.spre[...]
        for step in range(1, groups):
            g = lax.rem(plane + step, groups)
            remote(v.uout, v.ubuf.at[g], v.ux_s.at[step - 1], v.ux_r.at[g], sibling).wait_recv()
            rows = pl.ds(pl.multiple_of(g * picks, picks), picks)
            found = found - through(v.ubuf[g], (v.gz[0, rows], v.gz[1, rows]), dot)
        v.zbuf[core] = found
        for copy in z_copies:
            copy.start()
        for step in range(1, groups):
            g = lax.rem(plane + step, groups)
            rows = pl.ds(pl.multiple_of(g * picks, picks), picks)
            solved = solved - through(v.ubuf[g], (v.gs[0, rows], v.gs[1, rows]), dot)
        v.sol[core] = solved
        for copy in so_copies:
            copy.start()

    v.vin[...] = jnp.zeros_like(v.vin)

    def step_back(c):
        turned_copy(c, 0).wait_recv()
        if c == last:
            v.vin[...] = v.tbuf[c - 1]
        else:
            v.vin[...] = v.tbuf[c - 1] + through(v.vin[...], (v.later[c - 1, 0, 0], v.later[c - 1, 1, 0]), dot)

    from_later(chips, step_back)

    k_second = times(second - v.vin[...], fac[0, 1])
    k_first = times(first - times(k_second, fac[1, 1]), fac[0, 0])
    v.xs[0] = k_first
    v.xs[1] = k_second
    v.obuf[core] = v.xs[core]
    x_copy = remote(v.xs.at[other], v.obuf.at[core], v.x_s, v.x_r, sibling)
    x_copy.start()
    x_copy.wait_recv()

    def landed(buf, sem, k):
        pltpu.make_async_copy(buf.at[k], buf.at[k], sem.at[k]).wait()

    def arrivals(buf, sem):
        @pl.when(is_root)
        def _():
            landed(buf, sem, other)

        @pl.when(jnp.logical_not(is_root))
        def _():
            landed(buf, sem, 0)
            landed(buf, sem, 1)

    arrivals(v.zbuf, v.z_r)
    moved = through(v.zbuf[...].reshape(2 * half, picks), (v.fmap[core, 0], v.fmap[core, 1]), dot)
    out_ref[...] = v.obuf[...].reshape(out_ref.shape) - moved
    arrivals(v.sol, v.so_r)
    sol_ref[...] = v.sol[...].reshape(sol_ref.shape)

    for copy in swaps:
        copy.wait_send()
    sep_sends(lambda copy: copy.wait_send())

    @pl.when(jnp.logical_not(is_last))
    def _():
        y_copy.wait_send()

    @pl.when(chip < root)
    def _():
        u_copy.wait_send()

    @pl.when(is_last)
    def _():
        ul_copy.wait_send()
        s_copy.wait_send()

    to_earlier(last, lambda c, to: map_copy(c, to).wait_send())
    to_earlier(chips, lambda c, to: turned_copy(c, to).wait_send())
    from_later(last, lambda c: map_onward(c, core).wait_send())

    @pl.when(is_root)
    def _():
        s_onward.wait_send()
        peers(lambda g, to: id_copy(g, to, plane).wait_send())
        peers(lambda g, to: rs_copy(g, to, plane).wait_send())
        for g in range(groups):
            part = sep_part(g, core)
            remote(part, part, v.fwd_s.at[g], v.fwd_r.at[g], sibling).wait_send()
        for copy in u_copies + z_copies + so_copies:
            copy.wait_send()

    x_copy.wait_send()


def solution(mesh):
    groups, fronts = mesh.shape["leaf"], mesh.shape["front"]
    chips = fronts // 2

    def shards(rhs_leaf, diag_inv, sub_block, coupling, update_rows, rhs_sep, sep_inv):
        width, columns = rhs_leaf.shape[1:]
        picks = coupling.shape[1]
        wide = rhs_sep.shape[0]
        deep = sep_inv.shape[0]
        half = columns // 2
        skips = tuple(g * wide // (2 * deep) for g in range(groups))
        chunk = groups * picks if groups <= 4 else picks
        vmem, dma = pltpu.VMEM, pltpu.SemaphoreType.DMA
        scratch = dict(
            fac=vmem((3, 2, width, width), BF16),
            rown=vmem((columns, width), F32),
            rin=vmem((half, width), F32),
            maps=vmem((2, 2, width, width), BF16),
            slast=vmem((2, picks, width), BF16),
            later=vmem((chips - 2, 2, 2, width, width), BF16),
            tn=vmem((2, picks, width), BF16),
            fmap=vmem((2, 2, picks, width), BF16),
            tout=vmem((half, width), F32),
            tbuf=vmem((chips - 1, half, width), F32),
            yin=vmem((half, width), F32),
            yout=vmem((half, width), F32),
            uin=vmem((half, picks), F32),
            uout=vmem((half, picks), F32),
            ulast=vmem((half, picks), F32),
            upre=vmem((half, picks), F32),
            ubuf=vmem((groups, half, picks), F32),
            rsbuf=vmem((groups, half, wide), F32),
            idx=vmem((groups, 1, picks), jnp.int32),
            sep=vmem((groups, 2, chips, deep, wide), BF16),
            sel=vmem((groups * picks, groups * wide), BF16),
            at=vmem((chips, groups * picks, 2 * deep), BF16),
            gz=vmem((2, groups * picks, picks), BF16),
            gs=vmem((2, groups * picks, wide), BF16),
            zpre=vmem((half, picks), F32),
            spre=vmem((half, wide), F32),
            zbuf=vmem((2, half, picks), F32),
            sol=vmem((2, half, wide), F32),
            vin=vmem((half, width), F32),
            xs=vmem((2, half, width), F32),
            obuf=vmem((2, half, width), F32),
            up=pltpu.SemaphoreType.REGULAR,
            loc_s=dma((6,)), swap_s=dma((4,)), swap_r=dma((4,)),
            y_s=dma, y_r=dma, u_s=dma, u_r=dma, ul_r=dma, s_s=dma, s_r=dma, sf_s=dma, sf_r=dma,
            ux_s=dma((groups,)), ux_r=dma((groups,)), rs_s=dma((groups,)), rs_r=dma((groups,)),
            id_s=dma((groups,)), id_r=dma((groups,)), sep_s=dma((groups,)), sep_r=dma((groups,)),
            fwd_s=dma((groups,)), fwd_r=dma((groups,)),
            m_s=dma((chips,)), m_r=dma((chips,)), mf_s=dma((chips,)), mf_r=dma((chips,)),
            t_s=dma((chips,)), t_r=dma((chips,)),
            z_s=dma((2 * chips,)), z_r=dma((2,)), so_s=dma((2 * chips,)), so_r=dma((2,)),
            x_s=dma, x_r=dma,
        )
        out, sol = pl.pallas_call(
            functools.partial(kernel, groups, chips, skips, chunk, tuple(scratch)),
            out_shape=(vmem((columns, width), F32), vmem((columns, wide), F32)),
            in_specs=[pl.BlockSpec(memory_space=pltpu.HBM)] * 7,
            out_specs=(pl.BlockSpec(memory_space=vmem), pl.BlockSpec(memory_space=vmem)),
            scratch_shapes=list(scratch.values()),
            compiler_params=pltpu.CompilerParams(
                collective_id=0, has_side_effects=True, vmem_limit_bytes=65344 * 1024
            ),
        )(
            rhs_leaf[0].T, diag_inv[0, 0], sub_block[0, 0], coupling[0],
            update_rows, rhs_sep.T, sep_inv,
        )
        return out.T[None], sol.T

    return jax.shard_map(
        shards,
        mesh=mesh,
        in_specs=(
            P("leaf", "front", None),
            P("leaf", "front", None, None),
            P("leaf", "front", None, None),
            P("leaf", None, "front"),
            P("leaf", None),
            P("leaf", None),
            P("front", "leaf"),
        ),
        out_specs=(P("leaf", "front", None), P("leaf", None)),
        check_vma=False,
    )
```

```python
import functools
import types

import jax
import jax.numpy as jnp
from jax import lax
from jax.experimental import pallas as pl
from jax.experimental.pallas import tpu as pltpu
from jax.sharding import PartitionSpec as P

MESH = pl.DeviceIdType.MESH
F32 = jnp.float32
BF16 = jnp.bfloat16


def halves(x):
    head = x.astype(BF16)
    rest = (x - head.astype(F32)).astype(BF16)
    return jnp.concatenate([head, rest], axis=0)


def joined(both):
    rows = both.shape[0] // 2
    return both[:rows] + both[rows:]


def dot(a, b):
    return jnp.dot(a, b, preferred_element_type=F32)


def dot_t(a, b):
    return lax.dot_general(a, b, (((1,), (1,)), ((), ())), preferred_element_type=F32)


def times(x, w):
    return joined(dot(halves(x), w))


def times_t(x, w):
    return joined(dot_t(halves(x), w))


def split(x):
    head = x.astype(BF16)
    return head, (x - head.astype(F32)).astype(BF16)


def through(x, w, multiply):
    head, rest = w
    both = halves(x)
    return joined(multiply(both, head)) + multiply(both[: x.shape[0]], rest)


def composed(a, b):
    return dot(a[0], b[0]) + (dot(a[1], b[0]) + dot(a[0], b[1]))


def kernel(groups, chips, skips, names, r_ref, d_ref, b_ref, c_ref, idx_ref, rs_ref, sp_ref, out_ref, sol_ref, *refs):
    v = types.SimpleNamespace(**dict(zip(names, refs)))
    plane = lax.axis_index("leaf")
    front = lax.axis_index("front")
    chip = front // 2
    core = front % 2
    other = 1 - core
    last = chips - 1
    root = chips - 2
    is_root = chip == root
    is_last = chip == last
    is_mid = jnp.logical_and(chip > 0, chip < root)
    sibling = (plane, chip * 2 + other)
    half = v.yin.shape[0]
    picks = v.uin.shape[1]
    deep, wide = v.sep.shape[3:]
    fac = v.fac

    def remote(src, dst, send, recv, to):
        return pltpu.make_async_remote_copy(
            src_ref=src, dst_ref=dst, send_sem=send, recv_sem=recv, device_id=to, device_id_type=MESH
        )

    def near(c):
        return (plane, c * 2 + core)

    mine_rows = pl.ds(pl.multiple_of(core * half, half), half)
    other_rows = pl.ds(pl.multiple_of(other * half, half), half)

    barrier = pltpu.get_barrier_semaphore()

    def signal(sem, to):
        pl.semaphore_signal(sem, inc=1, device_id=to, device_id_type=MESH)

    signal(barrier, sibling)
    for c in range(chips):
        @pl.when(chip != c)
        def _(c=c):
            signal(barrier, near(c))
    for g in range(1, groups):
        @pl.when(plane < g)
        def _(g=g):
            @pl.when(is_root)
            def _():
                for c in range(chips):
                    signal(barrier, (g, c * 2 + core))

            @pl.when(jnp.logical_not(is_root))
            def _():
                signal(barrier, (g, root * 2 + core))

    loads = [pltpu.make_async_copy(r_ref, v.rown, v.loc_s.at[0])]
    for i, ref in enumerate((d_ref, b_ref, c_ref)):
        loads.append(pltpu.make_async_copy(ref, fac.at[i, core], v.loc_s.at[i + 1]))
    for copy in loads:
        copy.start()
    for copy in loads:
        copy.wait()

    pl.semaphore_wait(barrier, chips + jnp.where(is_root, plane * chips, plane))

    swaps = [remote(v.rown.at[other_rows], v.rin, v.swap_s.at[0], v.swap_r.at[0], sibling)]
    for i in range(3):
        part = fac.at[i, core]
        swaps.append(remote(part, part, v.swap_s.at[i + 1], v.swap_r.at[i + 1], sibling))
    for copy in swaps:
        copy.start()

    @pl.when(is_root)
    def _():
        for g in range(groups - 1):
            @pl.when(plane > g)
            def _(g=g):
                for c in range(chips):
                    signal(v.up, (g, c * 2 + core))

    for copy in swaps[:3]:
        copy.wait_recv()
    mine = v.rown[mine_rows]
    theirs = v.rin[...]
    r_first = jnp.where(core == 0, mine, theirs)
    r_second = jnp.where(core == 0, theirs, mine)

    y_copy = remote(v.yout, v.yin, v.y_s, v.y_r, near(jnp.minimum(chip + 1, root)))
    yl_copy = remote(v.yout, v.yin, v.yl_s, v.y_r, near(last))
    o_copy = remote(v.yout, v.oin, v.o_s, v.o_r, near(last))
    u_copy = remote(v.uout, v.uin, v.u_s, v.u_r, near(jnp.minimum(chip + 1, root)))
    pair_to = near(jnp.where(is_last, root, last))
    e_copy = remote(v.maps.at[jnp.where(is_last, 1, 0), core], v.edge.at[core], v.e_s, v.e_r, pair_to)
    e_onward = remote(v.edge.at[core], v.edge.at[core], v.ef_s, v.ef_r, sibling)
    e_theirs = remote(v.edge.at[other], v.edge.at[other], v.ef_s, v.ef_r, sibling)
    at_edge = chip >= root
    below = root - 1
    g_copy = remote(v.maps.at[1, core], v.far.at[0, core], v.g_s, v.g_r.at[0], near(below))
    h_copy = remote(v.maps.at[1, core], v.far.at[1, core], v.g_s, v.g_r.at[1], near(below))
    d_copy = remote(v.tout2.at[core], v.tn.at[core], v.d_s, v.d_r, near(jnp.maximum(chip - 1, 0)))

    def across(buf, k, send, recv):
        return remote(buf.at[k], buf.at[k], send, recv, sibling)

    def d_across(k):
        return across(v.tn, k, v.df_s, v.df_r)

    def far_across(i, k):
        return across(v.far.at[i], k, v.gf_s.at[i], v.gf_r.at[i])

    u_copies = []
    for step in range(1, groups):
        g = lax.rem(plane + step, groups)
        u_copies.append(
            remote(v.uout, v.ubuf.at[0, plane], v.ux_s.at[step], v.ux_r.at[0, plane], (g, root * 2 + core))
        )
    ul_copies = []
    for step in reversed(range(groups)):
        g = lax.rem(plane + step, groups)
        ul_copies.append(
            remote(v.uout, v.ubuf.at[1, plane], v.ux_s.at[step], v.ux_r.at[1, plane], (g, root * 2 + core))
        )

    own_first = times_t(r_first, fac[0, 0])
    own_second = times_t(r_second - times_t(own_first, fac[1, 1]), fac[0, 1])

    @pl.when(chip == 0)
    def _():
        v.yin[...] = jnp.zeros_like(v.yin)
        v.yout[...] = own_second
        y_copy.start()
        if root == 1:
            yl_copy.start()

    @pl.when(is_root)
    def _():
        v.yout[...] = own_second
        o_copy.start()

    @pl.when(plane < groups - 1)
    def _():
        pl.semaphore_wait(v.up, groups - 1 - plane)

    def sep_copy(g):
        return remote(sp_ref, v.sep.at[core, chip, plane], v.sep_s.at[g], v.sep_r.at[chip], (g, root * 2 + core))

    useful = chip >= (plane * wide) // (2 * deep)

    def sep_away(action):
        for g in reversed(range(groups)):
            @pl.when(jnp.logical_and(useful, plane != g))
            def _(g=g):
                action(sep_copy(g))

    def sep_near(action):
        for g in range(groups):
            @pl.when(jnp.logical_and(jnp.logical_and(useful, plane == g), jnp.logical_not(is_root)))
            def _(g=g):
                action(sep_copy(g))

    def peers(action):
        for g in range(groups):
            @pl.when(plane != g)
            def _(g=g):
                action(g, (g, root * 2 + core))

    def rs_copy(g, to, at):
        return remote(rs_ref.at[mine_rows], v.rsbuf.at[at], v.rs_s.at[g], v.rs_r.at[at], to)

    def id_copy(g, to, at):
        return remote(idx_ref, v.idx.at[at], v.id_s.at[g], v.id_r.at[at], to)

    own_rs = pltpu.make_async_copy(rs_ref.at[mine_rows], v.rsbuf.at[plane], v.loc_s.at[4])
    own_id = pltpu.make_async_copy(idx_ref, v.idx.at[plane], v.loc_s.at[5])

    @pl.when(is_root)
    def _():
        own_rs.start()
        own_id.start()
        peers(lambda g, to: id_copy(g, to, plane).start())
        peers(lambda g, to: rs_copy(g, to, plane).start())

        @pl.when(useful)
        def _():
            pltpu.make_async_copy(sp_ref, v.sep.at[core, root, plane], v.sep_r.at[root]).start()

    sep_away(lambda copy: copy.start())

    swaps[3].wait_recv()
    own_update = times_t(own_first, fac[2, 0]) + times_t(own_second, fac[2, 1])

    @pl.when(chip == 0)
    def _():
        v.uout[...] = own_update
        u_copy.start()

    early = split(dot(fac[0, 0], fac[1, 0]))
    late = split(dot(fac[0, 1], fac[1, 1]))
    whole = split(composed(late, early))
    for part in range(2):
        v.maps[0, part] = whole[part]

    @pl.when(is_root)
    def _():
        e_copy.start()

    seen = split(
        dot(fac[2, 1], whole[0]) - dot(fac[2, 0], early[0])
        + (dot(fac[2, 1], whole[1]) - dot(fac[2, 0], early[1]))
    )
    for part in range(2):
        v.maps[1, part] = seen[part]

    @pl.when(is_last)
    def _():
        g_copy.start()

    def map_copy(i, c, to):
        return remote(v.maps.at[i, core], v.later.at[c - 1, i, core], v.m_s.at[i, to], v.m_r.at[i, c - 1], near(to))

    def map_onward(i, c, k):
        part = v.later.at[c - 1, i, k]
        return remote(part, part, v.mf_s.at[i, c - 1], v.mf_r.at[i, c - 1], sibling)

    def turned_copy(c, to):
        return remote(v.tout, v.tbuf.at[c - 1], v.t_s.at[to], v.t_r.at[c - 1], near(to))

    def to_earlier(places, action):
        for c in places:
            @pl.when(chip == c)
            def _(c=c):
                for to in reversed(range(c)):
                    action(c, to)

    def from_later(places, action):
        for c in places:
            @pl.when(chip < c)
            def _(c=c):
                action(c)

    to_earlier([root], lambda c, to: map_copy(0, c, to).start())

    @pl.when(is_root)
    def _():
        h_copy.start()

    sep_near(lambda copy: copy.start())

    @pl.when(is_last)
    def _():
        e_copy.start()

    @pl.when(is_root)
    def _():
        for g in range(groups):
            for c in range(skips[g]):
                v.sep[:, c, g] = jnp.zeros((2, deep, wide), BF16)
        own_id.wait()
        own_rs.wait()
        peers(lambda g, to: id_copy(g, to, g).wait_recv())
        lanes = min(128, picks)
        for g in range(groups):
            index = jnp.transpose(jnp.broadcast_to(v.idx[g].astype(F32), (lanes, picks)))
            for at in range(0, groups * wide, lanes):
                column = lax.broadcasted_iota(jnp.int32, (picks, lanes), 1) + at
                v.sel[g * picks : (g + 1) * picks, at : at + lanes] = (
                    (index == column.astype(F32)).astype(F32).astype(BF16)
                )

    def edge_arrives():
        e_copy.wait_recv()
        e_onward.start()
        e_theirs.wait_recv()

    @pl.when(is_last)
    def _():
        edge_arrives()

    @pl.when(chip > 0)
    def _():
        y_copy.wait_recv()

    @pl.when(is_last)
    def _():
        o_copy.wait_recv()
        v.yin[...] = v.oin[...] + through(v.yin[...], (v.edge[0], v.edge[1]), dot_t)

    heard = v.yin[...]
    second = own_second + through(heard, whole, dot_t)

    @pl.when(is_mid)
    def _():
        v.yout[...] = second
        y_copy.start()

        @pl.when(chip == root - 1)
        def _():
            yl_copy.start()

        update = own_update + through(heard, seen, dot_t)
        u_copy.wait_recv()
        v.uout[...] = update + v.uin[...]
        u_copy.start()

    @pl.when(at_edge)
    def _():
        v.uout[...] = own_update + through(heard, seen, dot_t)

    @pl.when(is_last)
    def _():
        for copy in ul_copies:
            copy.start()

    @pl.when(is_root)
    def _():
        u_copy.wait_recv()
        v.uout[...] += v.uin[...]
        for copy in u_copies:
            copy.start()

    to_earlier(range(1, root), lambda c, to: map_copy(0, c, to).start())
    first = own_first - times_t(times_t(heard, fac[1, 0]), fac[0, 0])
    v.tout[...] = times(times(first, fac[0, 0]), fac[1, 0]) - through(second, whole, dot)
    to_earlier(range(1, chips), lambda c, to: turned_copy(c, to).start())

    def final_maps():
        back = split(dot(fac[2, 1], fac[0, 1]) + dot(v.tn[0], fac[0, 1]) + dot(v.tn[1], fac[0, 1]))
        between = split(dot(back[0], fac[1, 1]) + dot(back[1], fac[1, 1]))
        ahead = split(dot(fac[2, 0], fac[0, 0]) - (dot(between[0], fac[0, 0]) + dot(between[1], fac[0, 0])))
        for part in range(2):
            v.fmap[0, part] = ahead[part]
            v.fmap[1, part] = back[part]

    x_copy = remote(v.xs.at[other], v.obuf.at[core], v.x_s, v.x_r, sibling)

    def step_back(c):
        turned_copy(c, 0).wait_recv()
        if c == last:
            v.vin[...] = v.tbuf[c - 1]
        else:
            v.vin[...] = v.tbuf[c - 1] + through(v.vin[...], (v.later[c - 1, 0, 0], v.later[c - 1, 0, 1]), dot)

    def plain_part():
        v.vin[...] = jnp.zeros_like(v.vin)
        from_later(reversed(range(1, chips)), step_back)
        k_second = times(second - v.vin[...], fac[0, 1])
        k_first = times(first - times(k_second, fac[1, 1]), fac[0, 0])
        v.xs[0] = k_first
        v.xs[1] = k_second
        v.obuf[core] = v.xs[core]
        x_copy.start()

    def block(g, c):
        return jnp.concatenate([v.sep[0, c, g], v.sep[1, c, g]], axis=0)

    def sep_part(c, k):
        return v.sep.at[k, c, pl.ds(0, sum(skip <= c for skip in skips))]

    def sep_onward(c, k):
        return remote(sep_part(c, k), sep_part(c, k), v.fwd_s.at[c], v.fwd_r.at[c], sibling)

    own_rows = pl.ds(pl.multiple_of(plane * picks, picks), picks)
    targets = [near(c) for c in reversed(range(root))] + [near(last)]
    z_copies = [remote(v.zbuf.at[core], v.zbuf.at[core], v.z_s.at[i], v.z_r.at[core], to) for i, to in enumerate(targets)]
    so_copies = [remote(v.sol.at[core], v.sol.at[core], v.so_s.at[i], v.so_r.at[core], to) for i, to in enumerate(targets)]
    z_across = remote(v.zbuf.at[core], v.zbuf.at[core], v.z_s.at[chips], v.z_r.at[core], sibling)
    so_across = remote(v.sol.at[core], v.sol.at[core], v.so_s.at[chips], v.so_r.at[core], sibling)

    @pl.when(is_root)
    def _():
        for c in range(chips):
            pltpu.make_async_copy(sep_part(c, core), sep_part(c, core), v.sep_r.at[c]).wait()
            sep_onward(c, core).start()
        peers(lambda g, to: rs_copy(g, to, g).wait_recv())

        for c in range(chips):
            sep_onward(c, other).wait_recv()
            taken = 0
            for g in range(groups):
                if skips[g] <= c:
                    taken = taken + dot_t(v.sel[own_rows, g * wide : (g + 1) * wide], block(g, c))
            v.at[c] = taken.astype(BF16)

        def from_last(g):
            remote(v.uout, v.ubuf.at[1, g], v.ux_s.at[0], v.ux_r.at[1, g], sibling).wait_recv()

        from_last(plane)
        total = times(v.uout[...] + v.ubuf[1, plane], v.sel[own_rows])
        for step in range(1, groups):
            g = lax.rem(plane + step, groups)
            remote(v.uout, v.ubuf.at[0, g], v.ux_s.at[step], v.ux_r.at[0, g], sibling).wait_recv()
            from_last(g)
            rows = pl.ds(pl.multiple_of(g * picks, picks), picks)
            total = total + times(v.ubuf[0, g] + v.ubuf[1, g], v.sel[rows])
        parts = [halves(v.rsbuf[g] - total[:, g * wide : (g + 1) * wide]) for g in range(groups)]
        found, ahead = 0, []
        for c in range(chips):
            value = 0
            for g in range(groups):
                if skips[g] <= c:
                    value = value + dot_t(parts[g], block(g, c))
            ahead.append(halves(joined(value)))
            found = found + dot_t(ahead[c], v.at[c])
        v.zbuf[core] = joined(found)
        for copy in z_copies:
            copy.start()
        z_across.start()
        solved = 0
        for c in range(chips):
            solved = solved + dot(ahead[c], block(plane, c))
        v.sol[core] = joined(solved)
        for copy in so_copies:
            copy.start()
        so_across.start()
        plain_part()
        edge_arrives()
        for part in range(2):
            v.tn[part] = v.edge[part]
        final_maps()

    def pass_on(i, c):
        map_copy(i, c, 0).wait_recv()
        map_onward(i, c, core).start()

    def send_down():
        value = seen[0].astype(F32) + seen[1].astype(F32) + composed((v.tn[0], v.tn[1]), whole)
        for part, value in enumerate(split(value)):
            v.tout2[part] = value
        d_copy.start()

    @pl.when(jnp.logical_not(is_root))
    def _():
        from_later(reversed(range(1, last)), functools.partial(pass_on, 0))
        from_later(reversed(range(1, last)), lambda c: map_onward(0, c, other).wait_recv())

        @pl.when(chip == below)
        def _():
            h_copy.wait_recv()
            far_across(1, core).start()
            g_copy.wait_recv()
            far_across(0, core).start()
            far_across(1, other).wait_recv()
            far_across(0, other).wait_recv()
            value = v.far[1, 0].astype(F32) + v.far[1, 1].astype(F32) + composed(
                (v.far[0, 0], v.far[0, 1]), (v.later[root - 1, 0, 0], v.later[root - 1, 0, 1])
            )
            for part, value in enumerate(split(value)):
                v.tn[part] = value

            @pl.when(chip > 0)
            def _():
                send_down()

        plain_part()

        @pl.when(is_last)
        def _():
            v.tn[...] = jnp.zeros_like(v.tn)

        @pl.when(chip < below)
        def _():
            d_copy.wait_recv()
            d_across(core).start()
            d_across(other).wait_recv()

            @pl.when(chip > 0)
            def _():
                send_down()

        final_maps()

    x_copy.wait_recv()

    def solved_rows(k, rows):
        moved = through(v.zbuf[k], (v.fmap[core, 0], v.fmap[core, 1]), dot)
        out_ref[rows] = v.obuf[k] - moved

    @pl.when(jnp.logical_not(is_root))
    def _():
        z_copies[0].wait_recv()
        z_across.start()

    solved_rows(core, mine_rows)
    remote(v.zbuf.at[other], v.zbuf.at[other], v.z_s.at[chips], v.z_r.at[other], sibling).wait_recv()
    solved_rows(other, other_rows)

    @pl.when(jnp.logical_not(is_root))
    def _():
        so_copies[0].wait_recv()
        so_across.start()

    sol_ref[mine_rows] = v.sol[core]
    remote(v.sol.at[other], v.sol.at[other], v.so_s.at[chips], v.so_r.at[other], sibling).wait_recv()
    sol_ref[other_rows] = v.sol[other]

    for copy in swaps:
        copy.wait_send()
    sep_away(lambda copy: copy.wait_send())
    sep_near(lambda copy: copy.wait_send())

    @pl.when(chip < root)
    def _():
        y_copy.wait_send()
        u_copy.wait_send()

    @pl.when(chip == root - 1)
    def _():
        yl_copy.wait_send()

    @pl.when(at_edge)
    def _():
        e_copy.wait_send()
        e_onward.wait_send()

    @pl.when(is_last)
    def _():
        for copy in ul_copies:
            copy.wait_send()

    @pl.when(is_last)
    def _():
        g_copy.wait_send()

    @pl.when(is_root)
    def _():
        h_copy.wait_send()

    @pl.when(chip == below)
    def _():
        for i in range(2):
            far_across(i, core).wait_send()

    @pl.when(jnp.logical_and(chip > 0, chip < root))
    def _():
        d_copy.wait_send()

    @pl.when(chip < below)
    def _():
        d_across(core).wait_send()

    to_earlier(range(1, last), lambda c, to: map_copy(0, c, to).wait_send())
    from_later(range(1, last), lambda c: map_onward(0, c, core).wait_send())
    to_earlier(range(1, chips), lambda c, to: turned_copy(c, to).wait_send())

    @pl.when(is_root)
    def _():
        o_copy.wait_send()
        peers(lambda g, to: id_copy(g, to, plane).wait_send())
        peers(lambda g, to: rs_copy(g, to, plane).wait_send())
        for c in range(chips):
            sep_onward(c, core).wait_send()
        for copy in u_copies + z_copies + so_copies:
            copy.wait_send()

    x_copy.wait_send()
    z_across.wait_send()
    so_across.wait_send()


def solution(mesh):
    groups, fronts = mesh.shape["leaf"], mesh.shape["front"]
    chips = fronts // 2

    def shards(rhs_leaf, diag_inv, sub_block, coupling, update_rows, rhs_sep, sep_inv):
        width, columns = rhs_leaf.shape[1:]
        picks = coupling.shape[1]
        wide = rhs_sep.shape[0]
        deep = sep_inv.shape[0]
        half = columns // 2
        skips = tuple(g * wide // (2 * deep) for g in range(groups))
        vmem, dma = pltpu.VMEM, pltpu.SemaphoreType.DMA
        scratch = dict(
            fac=vmem((3, 2, width, width), BF16),
            rown=vmem((columns, width), F32),
            rin=vmem((half, width), F32),
            maps=vmem((2, 2, width, width), BF16),
            edge=vmem((2, width, width), BF16),
            later=vmem((chips - 2, 1, 2, width, width), BF16),
            far=vmem((2, 2, width, width), BF16),
            tout2=vmem((2, picks, width), BF16),
            tn=vmem((2, picks, width), BF16),
            fmap=vmem((2, 2, picks, width), BF16),
            tout=vmem((half, width), F32),
            tbuf=vmem((chips - 1, half, width), F32),
            yin=vmem((half, width), F32),
            yout=vmem((half, width), F32),
            oin=vmem((half, width), F32),
            uin=vmem((half, picks), F32),
            uout=vmem((half, picks), F32),
            ubuf=vmem((2, groups, half, picks), F32),
            rsbuf=vmem((groups, half, wide), F32),
            idx=vmem((groups, 1, picks), jnp.int32),
            sep=vmem((2, chips, groups, deep, wide), BF16),
            sel=vmem((groups * picks, groups * wide), BF16),
            at=vmem((chips, picks, 2 * deep), BF16),
            zbuf=vmem((2, half, picks), F32),
            sol=vmem((2, half, wide), F32),
            vin=vmem((half, width), F32),
            xs=vmem((2, half, width), F32),
            obuf=vmem((2, half, width), F32),
            up=pltpu.SemaphoreType.REGULAR,
            loc_s=dma((6,)), swap_s=dma((4,)), swap_r=dma((4,)),
            y_s=dma, y_r=dma, yl_s=dma, o_s=dma, o_r=dma, u_s=dma, u_r=dma,
            e_s=dma, e_r=dma, ef_s=dma, ef_r=dma,
            ux_s=dma((groups,)), ux_r=dma((2, groups)), rs_s=dma((groups,)), rs_r=dma((groups,)),
            id_s=dma((groups,)), id_r=dma((groups,)), sep_s=dma((groups,)), sep_r=dma((chips,)),
            fwd_s=dma((chips,)), fwd_r=dma((chips,)),
            m_s=dma((1, chips)), m_r=dma((1, chips)), mf_s=dma((1, chips)), mf_r=dma((1, chips)),
            g_s=dma, g_r=dma((2,)), gf_s=dma((2,)), gf_r=dma((2,)), d_s=dma, d_r=dma, df_s=dma, df_r=dma,
            t_s=dma((chips,)), t_r=dma((chips,)),
            z_s=dma((chips + 1,)), z_r=dma((2,)), so_s=dma((chips + 1,)), so_r=dma((2,)),
            x_s=dma, x_r=dma,
        )
        out, sol = pl.pallas_call(
            functools.partial(kernel, groups, chips, skips, tuple(scratch)),
            out_shape=(vmem((columns, width), F32), vmem((columns, wide), F32)),
            in_specs=[pl.BlockSpec(memory_space=pltpu.HBM)] * 7,
            out_specs=(pl.BlockSpec(memory_space=vmem), pl.BlockSpec(memory_space=vmem)),
            scratch_shapes=list(scratch.values()),
            compiler_params=pltpu.CompilerParams(
                collective_id=0, has_side_effects=True, vmem_limit_bytes=65344 * 1024
            ),
        )(
            rhs_leaf[0].T, diag_inv[0, 0], sub_block[0, 0], coupling[0],
            update_rows, rhs_sep.T, sep_inv,
        )
        return out.T[None], sol.T

    return jax.shard_map(
        shards,
        mesh=mesh,
        in_specs=(
            P("leaf", "front", None),
            P("leaf", "front", None, None),
            P("leaf", "front", None, None),
            P("leaf", None, "front"),
            P("leaf", None),
            P("leaf", None),
            P("front", "leaf"),
        ),
        out_specs=(P("leaf", "front", None), P("leaf", None)),
        check_vma=False,
    )
```

```python
import functools
import types

import jax
import jax.numpy as jnp
from jax import lax
from jax.experimental import pallas as pl
from jax.experimental.pallas import tpu as pltpu
from jax.sharding import PartitionSpec as P

MESH = pl.DeviceIdType.MESH
F32 = jnp.float32
BF16 = jnp.bfloat16


def halves(x):
    head = x.astype(BF16)
    rest = (x - head.astype(F32)).astype(BF16)
    return jnp.concatenate([head, rest], axis=0)


def joined(both):
    rows = both.shape[0] // 2
    return both[:rows] + both[rows:]


def dot(a, b):
    return jnp.dot(a, b, preferred_element_type=F32)


def dot_t(a, b):
    return lax.dot_general(a, b, (((1,), (1,)), ((), ())), preferred_element_type=F32)


def times(x, w):
    return joined(dot(halves(x), w))


def times_t(x, w):
    return joined(dot_t(halves(x), w))


def split(x):
    head = x.astype(BF16)
    return head, (x - head.astype(F32)).astype(BF16)


def through(x, w, multiply):
    head, rest = w
    both = halves(x)
    return joined(multiply(both, head)) + multiply(both[: x.shape[0]], rest)


def composed(a, b):
    return dot(a[0], b[0]) + (dot(a[1], b[0]) + dot(a[0], b[1]))


def kernel(groups, chips, skips, names, r_ref, d_ref, b_ref, c_ref, idx_ref, rs_ref, sp_ref, out_ref, sol_ref, *refs):
    v = types.SimpleNamespace(**dict(zip(names, refs)))
    plane = lax.axis_index("leaf")
    front = lax.axis_index("front")
    chip = front // 2
    core = front % 2
    other = 1 - core
    last = chips - 1
    root = chips - 2
    is_root = chip == root
    is_last = chip == last
    is_mid = jnp.logical_and(chip > 0, chip < root)
    sibling = (plane, chip * 2 + other)
    half = v.yin.shape[0]
    picks = v.uin.shape[1]
    deep, wide = v.sep.shape[3:]
    fac = v.fac

    def remote(src, dst, send, recv, to):
        return pltpu.make_async_remote_copy(
            src_ref=src, dst_ref=dst, send_sem=send, recv_sem=recv, device_id=to, device_id_type=MESH
        )

    def near(c):
        return (plane, c * 2 + core)

    mine_rows = pl.ds(pl.multiple_of(core * half, half), half)
    other_rows = pl.ds(pl.multiple_of(other * half, half), half)

    barrier = pltpu.get_barrier_semaphore()

    def signal(sem, to):
        pl.semaphore_signal(sem, inc=1, device_id=to, device_id_type=MESH)

    signal(barrier, sibling)
    for c in range(chips):
        @pl.when(chip != c)
        def _(c=c):
            signal(barrier, near(c))
    for g in range(1, groups):
        @pl.when(plane < g)
        def _(g=g):
            @pl.when(is_root)
            def _():
                for c in range(chips):
                    signal(barrier, (g, c * 2 + core))

            @pl.when(jnp.logical_not(is_root))
            def _():
                signal(barrier, (g, root * 2 + core))

    loads = [pltpu.make_async_copy(r_ref, v.rown, v.loc_s.at[0])]
    for i, ref in enumerate((d_ref, b_ref, c_ref)):
        loads.append(pltpu.make_async_copy(ref, fac.at[i, core], v.loc_s.at[i + 1]))
    for copy in loads:
        copy.start()
    for copy in loads:
        copy.wait()

    pl.semaphore_wait(barrier, chips + jnp.where(is_root, plane * chips, plane))

    swaps = [remote(v.rown.at[other_rows], v.rin, v.swap_s.at[0], v.swap_r.at[0], sibling)]
    for i in range(3):
        part = fac.at[i, core]
        swaps.append(remote(part, part, v.swap_s.at[i + 1], v.swap_r.at[i + 1], sibling))
    for copy in swaps:
        copy.start()

    @pl.when(is_root)
    def _():
        for g in range(groups - 1):
            @pl.when(plane > g)
            def _(g=g):
                for c in range(chips):
                    signal(v.up, (g, c * 2 + core))

    for copy in swaps[:3]:
        copy.wait_recv()
    mine = v.rown[mine_rows]
    theirs = v.rin[...]
    r_first = jnp.where(core == 0, mine, theirs)
    r_second = jnp.where(core == 0, theirs, mine)

    y_copy = remote(v.yout, v.yin, v.y_s, v.y_r, near(jnp.minimum(chip + 1, root)))
    yl_copy = remote(v.yout, v.yin, v.yl_s, v.y_r, near(last))
    o_copy = remote(v.yout, v.oin, v.o_s, v.o_r, near(last))
    u_copy = remote(v.uout, v.uin, v.u_s, v.u_r, near(jnp.minimum(chip + 1, root)))
    pair_to = near(jnp.where(is_last, root, last))
    e_copy = remote(v.maps.at[jnp.where(is_last, 1, 0), core], v.edge.at[core], v.e_s, v.e_r, pair_to)
    e_onward = remote(v.edge.at[core], v.edge.at[core], v.ef_s, v.ef_r, sibling)
    e_theirs = remote(v.edge.at[other], v.edge.at[other], v.ef_s, v.ef_r, sibling)
    at_edge = chip >= root
    below = root - 1
    g_copy = remote(v.maps.at[1, core], v.far.at[0, core], v.g_s, v.g_r.at[0], near(below))
    h_copy = remote(v.maps.at[1, core], v.far.at[1, core], v.g_s, v.g_r.at[1], near(below))
    d_copy = remote(v.tout2.at[core], v.tn.at[core], v.d_s, v.d_r, near(jnp.maximum(chip - 1, 0)))

    def across(buf, k, send, recv):
        return remote(buf.at[k], buf.at[k], send, recv, sibling)

    def d_across(k):
        return across(v.tn, k, v.df_s, v.df_r)

    def far_across(i, k):
        return across(v.far.at[i], k, v.gf_s.at[i], v.gf_r.at[i])

    u_copies = []
    for step in range(1, groups):
        g = lax.rem(plane + step, groups)
        u_copies.append(
            remote(v.uout, v.ubuf.at[0, plane], v.ux_s.at[step], v.ux_r.at[0, plane], (g, root * 2 + core))
        )
    ul_copies = []
    for step in reversed(range(groups)):
        g = lax.rem(plane + step, groups)
        ul_copies.append(
            remote(v.uout, v.ubuf.at[1, plane], v.ux_s.at[step], v.ux_r.at[1, plane], (g, root * 2 + core))
        )

    own_first = times_t(r_first, fac[0, 0])
    own_second = times_t(r_second - times_t(own_first, fac[1, 1]), fac[0, 1])

    @pl.when(chip == 0)
    def _():
        v.yin[...] = jnp.zeros_like(v.yin)
        v.yout[...] = own_second
        y_copy.start()
        if root == 1:
            yl_copy.start()

    @pl.when(is_root)
    def _():
        v.yout[...] = own_second
        o_copy.start()

    @pl.when(plane < groups - 1)
    def _():
        pl.semaphore_wait(v.up, groups - 1 - plane)

    def sep_copy(g):
        return remote(sp_ref, v.sep.at[core, chip, plane], v.sep_s.at[g], v.sep_r.at[chip], (g, root * 2 + core))

    useful = chip >= (plane * wide) // (2 * deep)

    def sep_away(action):
        for g in reversed(range(groups)):
            @pl.when(jnp.logical_and(useful, plane != g))
            def _(g=g):
                action(sep_copy(g))

    def sep_near(action):
        for g in range(groups):
            @pl.when(jnp.logical_and(jnp.logical_and(useful, plane == g), jnp.logical_not(is_root)))
            def _(g=g):
                action(sep_copy(g))

    def peers(action):
        for g in range(groups):
            @pl.when(plane != g)
            def _(g=g):
                action(g, (g, root * 2 + core))

    def rs_copy(g, to, at):
        return remote(rs_ref.at[mine_rows], v.rsbuf.at[at], v.rs_s.at[g], v.rs_r.at[at], to)

    def id_copy(g, to, at):
        return remote(idx_ref, v.idx.at[at], v.id_s.at[g], v.id_r.at[at], to)

    own_rs = pltpu.make_async_copy(rs_ref.at[mine_rows], v.rsbuf.at[plane], v.loc_s.at[4])
    own_id = pltpu.make_async_copy(idx_ref, v.idx.at[plane], v.loc_s.at[5])

    @pl.when(is_root)
    def _():
        own_rs.start()
        own_id.start()
        peers(lambda g, to: id_copy(g, to, plane).start())
        peers(lambda g, to: rs_copy(g, to, plane).start())

        @pl.when(useful)
        def _():
            pltpu.make_async_copy(sp_ref, v.sep.at[core, root, plane], v.sep_r.at[root]).start()

    sep_away(lambda copy: copy.start())

    swaps[3].wait_recv()
    own_update = times_t(own_first, fac[2, 0]) + times_t(own_second, fac[2, 1])

    @pl.when(chip == 0)
    def _():
        v.uout[...] = own_update
        u_copy.start()

    early = split(dot(fac[0, 0], fac[1, 0]))
    late = split(dot(fac[0, 1], fac[1, 1]))
    whole = split(composed(late, early))
    for part in range(2):
        v.maps[0, part] = whole[part]

    @pl.when(is_root)
    def _():
        e_copy.start()

    seen = split(
        dot(fac[2, 1], whole[0]) - dot(fac[2, 0], early[0])
        + (dot(fac[2, 1], whole[1]) - dot(fac[2, 0], early[1]))
    )
    for part in range(2):
        v.maps[1, part] = seen[part]

    @pl.when(is_last)
    def _():
        g_copy.start()

    def map_copy(i, c, to):
        return remote(v.maps.at[i, core], v.later.at[c - 1, i, core], v.m_s.at[i, to], v.m_r.at[i, c - 1], near(to))

    def map_onward(i, c, k):
        part = v.later.at[c - 1, i, k]
        return remote(part, part, v.mf_s.at[i, c - 1], v.mf_r.at[i, c - 1], sibling)

    def turned_copy(c, to):
        return remote(v.tout, v.tbuf.at[c - 1], v.t_s.at[to], v.t_r.at[c - 1], near(to))

    def to_earlier(places, action):
        for c in places:
            @pl.when(chip == c)
            def _(c=c):
                for to in reversed(range(c)):
                    action(c, to)

    def from_later(places, action):
        for c in places:
            @pl.when(chip < c)
            def _(c=c):
                action(c)

    to_earlier([root], lambda c, to: map_copy(0, c, to).start())

    @pl.when(is_root)
    def _():
        h_copy.start()

    sep_near(lambda copy: copy.start())

    @pl.when(is_last)
    def _():
        e_copy.start()

    @pl.when(is_root)
    def _():
        for g in range(groups):
            for c in range(skips[g]):
                v.sep[:, c, g] = jnp.zeros((2, deep, wide), BF16)
        own_id.wait()
        own_rs.wait()
        peers(lambda g, to: id_copy(g, to, g).wait_recv())
        lanes = min(128, picks)
        for g in range(groups):
            index = jnp.transpose(jnp.broadcast_to(v.idx[g].astype(F32), (lanes, picks)))
            for at in range(0, groups * wide, lanes):
                column = lax.broadcasted_iota(jnp.int32, (picks, lanes), 1) + at
                v.sel[g * picks : (g + 1) * picks, at : at + lanes] = (
                    (index == column.astype(F32)).astype(F32).astype(BF16)
                )

    def edge_arrives():
        e_copy.wait_recv()
        e_onward.start()
        e_theirs.wait_recv()

    @pl.when(is_last)
    def _():
        edge_arrives()

    @pl.when(chip > 0)
    def _():
        y_copy.wait_recv()

    @pl.when(is_last)
    def _():
        o_copy.wait_recv()
        v.yin[...] = v.oin[...] + through(v.yin[...], (v.edge[0], v.edge[1]), dot_t)

    heard = v.yin[...]
    second = own_second + through(heard, whole, dot_t)

    @pl.when(is_mid)
    def _():
        v.yout[...] = second
        y_copy.start()

        @pl.when(chip == root - 1)
        def _():
            yl_copy.start()

        update = own_update + through(heard, seen, dot_t)
        u_copy.wait_recv()
        v.uout[...] = update + v.uin[...]
        u_copy.start()

    @pl.when(at_edge)
    def _():
        v.uout[...] = own_update + through(heard, seen, dot_t)

    @pl.when(is_last)
    def _():
        for copy in ul_copies:
            copy.start()

    @pl.when(is_root)
    def _():
        u_copy.wait_recv()
        v.uout[...] += v.uin[...]
        for copy in u_copies:
            copy.start()

    to_earlier(range(1, root), lambda c, to: map_copy(0, c, to).start())
    first = own_first - times_t(times_t(heard, fac[1, 0]), fac[0, 0])
    v.tout[...] = times(times(first, fac[0, 0]), fac[1, 0]) - through(second, whole, dot)
    to_earlier(range(1, chips), lambda c, to: turned_copy(c, to).start())

    def final_maps():
        back = split(dot(fac[2, 1], fac[0, 1]) + dot(v.tn[0], fac[0, 1]) + dot(v.tn[1], fac[0, 1]))
        between = split(dot(back[0], fac[1, 1]) + dot(back[1], fac[1, 1]))
        ahead = split(dot(fac[2, 0], fac[0, 0]) - (dot(between[0], fac[0, 0]) + dot(between[1], fac[0, 0])))
        for part in range(2):
            v.fmap[0, part] = ahead[part]
            v.fmap[1, part] = back[part]

    x_copy = remote(v.xs.at[other], v.obuf.at[core], v.x_s, v.x_r, sibling)

    def step_back(c):
        turned_copy(c, 0).wait_recv()
        if c == last:
            v.vin[...] = v.tbuf[c - 1]
        else:
            v.vin[...] = v.tbuf[c - 1] + through(v.vin[...], (v.later[c - 1, 0, 0], v.later[c - 1, 0, 1]), dot)

    def plain_part():
        v.vin[...] = jnp.zeros_like(v.vin)
        from_later(reversed(range(1, chips)), step_back)
        k_second = times(second - v.vin[...], fac[0, 1])
        k_first = times(first - times(k_second, fac[1, 1]), fac[0, 0])
        v.xs[0] = k_first
        v.xs[1] = k_second
        v.obuf[core] = v.xs[core]
        x_copy.start()

    def block(g, c):
        return jnp.concatenate([v.sep[0, c, g], v.sep[1, c, g]], axis=0)

    def sep_part(c, k):
        return v.sep.at[k, c, pl.ds(0, sum(skip <= c for skip in skips))]

    def sep_onward(c, k):
        return remote(sep_part(c, k), sep_part(c, k), v.fwd_s.at[c], v.fwd_r.at[c], sibling)

    own_rows = pl.ds(pl.multiple_of(plane * picks, picks), picks)
    targets = [near(c) for c in reversed(range(root))] + [near(last)]
    z_copies = [remote(v.zbuf.at[core], v.zbuf.at[core], v.z_s.at[i], v.z_r.at[core], to) for i, to in enumerate(targets)]
    so_copies = [remote(v.sol.at[core], v.sol.at[core], v.so_s.at[i], v.so_r.at[core], to) for i, to in enumerate(targets)]
    z_across = remote(v.zbuf.at[core], v.zbuf.at[core], v.z_s.at[chips], v.z_r.at[core], sibling)
    so_across = remote(v.sol.at[core], v.sol.at[core], v.so_s.at[chips], v.so_r.at[core], sibling)

    @pl.when(is_root)
    def _():
        for c in range(chips):
            pltpu.make_async_copy(sep_part(c, core), sep_part(c, core), v.sep_r.at[c]).wait()
            sep_onward(c, core).start()
        peers(lambda g, to: rs_copy(g, to, g).wait_recv())

        for c in range(chips):
            sep_onward(c, other).wait_recv()
            taken = 0
            for g in range(groups):
                if skips[g] <= c:
                    taken = taken + dot_t(v.sel[own_rows, g * wide : (g + 1) * wide], block(g, c))
            v.at[c] = taken.astype(BF16)

        def from_last(g):
            remote(v.uout, v.ubuf.at[1, g], v.ux_s.at[0], v.ux_r.at[1, g], sibling).wait_recv()

        from_last(plane)
        total = times(v.uout[...] + v.ubuf[1, plane], v.sel[own_rows])
        for step in range(1, groups):
            g = lax.rem(plane + step, groups)
            remote(v.uout, v.ubuf.at[0, g], v.ux_s.at[step], v.ux_r.at[0, g], sibling).wait_recv()
            from_last(g)
            rows = pl.ds(pl.multiple_of(g * picks, picks), picks)
            total = total + times(v.ubuf[0, g] + v.ubuf[1, g], v.sel[rows])
        parts = [halves(v.rsbuf[g] - total[:, g * wide : (g + 1) * wide]) for g in range(groups)]
        found, ahead = 0, []
        for c in range(chips):
            value = 0
            for g in range(groups):
                if skips[g] <= c:
                    value = value + dot_t(parts[g], block(g, c))
            ahead.append(halves(joined(value)))
            found = found + dot_t(ahead[c], v.at[c])
        v.zbuf[core] = joined(found)
        for copy in z_copies:
            copy.start()
        z_across.start()
        solved = 0
        for c in range(chips):
            solved = solved + dot(ahead[c], block(plane, c))
        v.sol[core] = joined(solved)
        for copy in so_copies:
            copy.start()
        so_across.start()
        plain_part()
        edge_arrives()
        for part in range(2):
            v.tn[part] = v.edge[part]
        final_maps()

    def pass_on(i, c):
        map_copy(i, c, 0).wait_recv()
        map_onward(i, c, core).start()

    def send_down():
        value = seen[0].astype(F32) + seen[1].astype(F32) + composed((v.tn[0], v.tn[1]), whole)
        for part, value in enumerate(split(value)):
            v.tout2[part] = value
        d_copy.start()

    @pl.when(jnp.logical_not(is_root))
    def _():
        @pl.when(chip == below)
        def _():
            g_copy.wait_recv()
            far_across(0, core).start()

        from_later(reversed(range(1, last)), functools.partial(pass_on, 0))

        @pl.when(chip == below)
        def _():
            h_copy.wait_recv()
            far_across(1, core).start()

        from_later(reversed(range(1, last)), lambda c: map_onward(0, c, other).wait_recv())

        @pl.when(chip == below)
        def _():
            far_across(0, other).wait_recv()
            far_across(1, other).wait_recv()
            value = v.far[1, 0].astype(F32) + v.far[1, 1].astype(F32) + composed(
                (v.far[0, 0], v.far[0, 1]), (v.later[root - 1, 0, 0], v.later[root - 1, 0, 1])
            )
            for part, value in enumerate(split(value)):
                v.tn[part] = value

            @pl.when(chip > 0)
            def _():
                send_down()

        plain_part()

        @pl.when(is_last)
        def _():
            v.tn[...] = jnp.zeros_like(v.tn)

        @pl.when(chip < below)
        def _():
            d_copy.wait_recv()
            d_across(core).start()
            d_across(other).wait_recv()

            @pl.when(chip > 0)
            def _():
                send_down()

        final_maps()

    x_copy.wait_recv()

    def solved_rows(k, rows):
        moved = through(v.zbuf[k], (v.fmap[core, 0], v.fmap[core, 1]), dot)
        out_ref[rows] = v.obuf[k] - moved

    @pl.when(jnp.logical_not(is_root))
    def _():
        z_copies[0].wait_recv()
        z_across.start()

    solved_rows(core, mine_rows)
    remote(v.zbuf.at[other], v.zbuf.at[other], v.z_s.at[chips], v.z_r.at[other], sibling).wait_recv()
    solved_rows(other, other_rows)

    @pl.when(jnp.logical_not(is_root))
    def _():
        so_copies[0].wait_recv()
        so_across.start()

    sol_ref[mine_rows] = v.sol[core]
    remote(v.sol.at[other], v.sol.at[other], v.so_s.at[chips], v.so_r.at[other], sibling).wait_recv()
    sol_ref[other_rows] = v.sol[other]

    for copy in swaps:
        copy.wait_send()
    sep_away(lambda copy: copy.wait_send())
    sep_near(lambda copy: copy.wait_send())

    @pl.when(chip < root)
    def _():
        y_copy.wait_send()
        u_copy.wait_send()

    @pl.when(chip == root - 1)
    def _():
        yl_copy.wait_send()

    @pl.when(at_edge)
    def _():
        e_copy.wait_send()
        e_onward.wait_send()

    @pl.when(is_last)
    def _():
        for copy in ul_copies:
            copy.wait_send()

    @pl.when(is_last)
    def _():
        g_copy.wait_send()

    @pl.when(is_root)
    def _():
        h_copy.wait_send()

    @pl.when(chip == below)
    def _():
        for i in range(2):
            far_across(i, core).wait_send()

    @pl.when(jnp.logical_and(chip > 0, chip < root))
    def _():
        d_copy.wait_send()

    @pl.when(chip < below)
    def _():
        d_across(core).wait_send()

    to_earlier(range(1, last), lambda c, to: map_copy(0, c, to).wait_send())
    from_later(range(1, last), lambda c: map_onward(0, c, core).wait_send())
    to_earlier(range(1, chips), lambda c, to: turned_copy(c, to).wait_send())

    @pl.when(is_root)
    def _():
        o_copy.wait_send()
        peers(lambda g, to: id_copy(g, to, plane).wait_send())
        peers(lambda g, to: rs_copy(g, to, plane).wait_send())
        for c in range(chips):
            sep_onward(c, core).wait_send()
        for copy in u_copies + z_copies + so_copies:
            copy.wait_send()

    x_copy.wait_send()
    z_across.wait_send()
    so_across.wait_send()


def store(x_ref, s_ref, out_ref, sol_ref, sems):
    copies = [
        pltpu.make_async_copy(x_ref, out_ref, sems.at[0]),
        pltpu.make_async_copy(s_ref, sol_ref, sems.at[1]),
    ]
    for copy in copies:
        copy.start()
    for copy in copies:
        copy.wait()


def solution(mesh):
    groups, fronts = mesh.shape["leaf"], mesh.shape["front"]
    chips = fronts // 2

    def shards(rhs_leaf, diag_inv, sub_block, coupling, update_rows, rhs_sep, sep_inv):
        width, columns = rhs_leaf.shape[1:]
        picks = coupling.shape[1]
        wide = rhs_sep.shape[0]
        deep = sep_inv.shape[0]
        half = columns // 2
        skips = tuple(g * wide // (2 * deep) for g in range(groups))
        vmem, dma = pltpu.VMEM, pltpu.SemaphoreType.DMA
        scratch = dict(
            fac=vmem((3, 2, width, width), BF16),
            rown=vmem((columns, width), F32),
            rin=vmem((half, width), F32),
            maps=vmem((2, 2, width, width), BF16),
            edge=vmem((2, width, width), BF16),
            later=vmem((chips - 2, 1, 2, width, width), BF16),
            far=vmem((2, 2, width, width), BF16),
            tout2=vmem((2, picks, width), BF16),
            tn=vmem((2, picks, width), BF16),
            fmap=vmem((2, 2, picks, width), BF16),
            tout=vmem((half, width), F32),
            tbuf=vmem((chips - 1, half, width), F32),
            yin=vmem((half, width), F32),
            yout=vmem((half, width), F32),
            oin=vmem((half, width), F32),
            uin=vmem((half, picks), F32),
            uout=vmem((half, picks), F32),
            ubuf=vmem((2, groups, half, picks), F32),
            rsbuf=vmem((groups, half, wide), F32),
            idx=vmem((groups, 1, picks), jnp.int32),
            sep=vmem((2, chips, groups, deep, wide), BF16),
            sel=vmem((groups * picks, groups * wide), BF16),
            at=vmem((chips, picks, 2 * deep), BF16),
            zbuf=vmem((2, half, picks), F32),
            sol=vmem((2, half, wide), F32),
            vin=vmem((half, width), F32),
            xs=vmem((2, half, width), F32),
            obuf=vmem((2, half, width), F32),
            up=pltpu.SemaphoreType.REGULAR,
            loc_s=dma((6,)), swap_s=dma((4,)), swap_r=dma((4,)),
            y_s=dma, y_r=dma, yl_s=dma, o_s=dma, o_r=dma, u_s=dma, u_r=dma,
            e_s=dma, e_r=dma, ef_s=dma, ef_r=dma,
            ux_s=dma((groups,)), ux_r=dma((2, groups)), rs_s=dma((groups,)), rs_r=dma((groups,)),
            id_s=dma((groups,)), id_r=dma((groups,)), sep_s=dma((groups,)), sep_r=dma((chips,)),
            fwd_s=dma((chips,)), fwd_r=dma((chips,)),
            m_s=dma((1, chips)), m_r=dma((1, chips)), mf_s=dma((1, chips)), mf_r=dma((1, chips)),
            g_s=dma, g_r=dma((2,)), gf_s=dma((2,)), gf_r=dma((2,)), d_s=dma, d_r=dma, df_s=dma, df_r=dma,
            t_s=dma((chips,)), t_r=dma((chips,)),
            z_s=dma((chips + 1,)), z_r=dma((2,)), so_s=dma((chips + 1,)), so_r=dma((2,)),
            x_s=dma, x_r=dma,
        )
        out, sol = pl.pallas_call(
            functools.partial(kernel, groups, chips, skips, tuple(scratch)),
            out_shape=(vmem((columns, width), F32), vmem((columns, wide), F32)),
            in_specs=[pl.BlockSpec(memory_space=pltpu.HBM)] * 7,
            out_specs=(pl.BlockSpec(memory_space=vmem), pl.BlockSpec(memory_space=vmem)),
            scratch_shapes=list(scratch.values()),
            compiler_params=pltpu.CompilerParams(
                collective_id=0, has_side_effects=True, vmem_limit_bytes=65344 * 1024
            ),
        )(
            rhs_leaf[0].T, diag_inv[0, 0], sub_block[0, 0], coupling[0],
            update_rows, rhs_sep.T, sep_inv,
        )
        hbm = pl.BlockSpec(memory_space=pltpu.HBM)
        out, sol = pl.pallas_call(
            store,
            out_shape=(
                jax.ShapeDtypeStruct((columns, width), F32),
                jax.ShapeDtypeStruct((columns, wide), F32),
            ),
            in_specs=[pl.BlockSpec(memory_space=vmem)] * 2,
            out_specs=(hbm, hbm),
            scratch_shapes=[dma((2,))],
            compiler_params=pltpu.CompilerParams(vmem_limit_bytes=1024 * 1024),
        )(out, sol)
        return out.T[None], sol.T

    return jax.shard_map(
        shards,
        mesh=mesh,
        in_specs=(
            P("leaf", "front", None),
            P("leaf", "front", None, None),
            P("leaf", "front", None, None),
            P("leaf", None, "front"),
            P("leaf", None),
            P("leaf", None),
            P("front", "leaf"),
        ),
        out_specs=(P("leaf", "front", None), P("leaf", None)),
        check_vma=False,
    )
```

```python
import functools
import types

import jax
import jax.numpy as jnp
from jax import lax
from jax.experimental import pallas as pl
from jax.experimental.pallas import tpu as pltpu
from jax.sharding import PartitionSpec as P

MESH = pl.DeviceIdType.MESH
F32 = jnp.float32
BF16 = jnp.bfloat16


def halves(x):
    head = x.astype(BF16)
    rest = (x - head.astype(F32)).astype(BF16)
    return jnp.concatenate([head, rest], axis=0)


def joined(both):
    rows = both.shape[0] // 2
    return both[:rows] + both[rows:]


def dot(a, b):
    return jnp.dot(a, b, preferred_element_type=F32)


def dot_t(a, b):
    return lax.dot_general(a, b, (((1,), (1,)), ((), ())), preferred_element_type=F32)


def times(x, w):
    return joined(dot(halves(x), w))


def times_t(x, w):
    return joined(dot_t(halves(x), w))


def split(x):
    head = x.astype(BF16)
    return head, (x - head.astype(F32)).astype(BF16)


def through(x, w, multiply):
    head, rest = w
    both = halves(x)
    return joined(multiply(both, head)) + multiply(both[: x.shape[0]], rest)


def composed(a, b):
    return dot(a[0], b[0]) + (dot(a[1], b[0]) + dot(a[0], b[1]))


def kernel(groups, chips, skips, names, r_ref, d_ref, b_ref, c_ref, idx_ref, rs_ref, sp_ref, out_ref, sol_ref, *refs):
    v = types.SimpleNamespace(**dict(zip(names, refs)))
    plane = lax.axis_index("leaf")
    front = lax.axis_index("front")
    chip = front // 2
    core = front % 2
    other = 1 - core
    last = chips - 1
    root = chips - 2
    is_root = chip == root
    is_last = chip == last
    is_mid = jnp.logical_and(chip > 0, chip < root)
    sibling = (plane, chip * 2 + other)
    half = v.yin.shape[0]
    picks = v.uin.shape[1]
    deep, wide = v.sep.shape[3:]
    fac = v.fac

    def remote(src, dst, send, recv, to):
        return pltpu.make_async_remote_copy(
            src_ref=src, dst_ref=dst, send_sem=send, recv_sem=recv, device_id=to, device_id_type=MESH
        )

    def near(c):
        return (plane, c * 2 + core)

    mine_rows = pl.ds(pl.multiple_of(core * half, half), half)
    other_rows = pl.ds(pl.multiple_of(other * half, half), half)

    barrier = pltpu.get_barrier_semaphore()

    def signal(sem, to):
        pl.semaphore_signal(sem, inc=1, device_id=to, device_id_type=MESH)

    signal(barrier, sibling)
    for c in range(chips):
        @pl.when(chip != c)
        def _(c=c):
            signal(barrier, near(c))
    for g in range(1, groups):
        @pl.when(plane < g)
        def _(g=g):
            @pl.when(is_root)
            def _():
                for c in range(chips):
                    signal(barrier, (g, c * 2 + core))

            @pl.when(jnp.logical_not(is_root))
            def _():
                signal(barrier, (g, root * 2 + core))

    @pl.when(chip < root)
    def _():
        edge_at = fac.shape[2] // 2
        for c in range(chips - 2):
            for k in range(2):
                v.later[c, 0, k, :edge_at, edge_at:] = jnp.zeros((edge_at, fac.shape[2] - edge_at), BF16)

    loads = [pltpu.make_async_copy(r_ref, v.rown, v.loc_s.at[0])]
    for i, ref in enumerate((d_ref, b_ref, c_ref)):
        loads.append(pltpu.make_async_copy(ref, fac.at[i, core], v.loc_s.at[i + 1]))
    for copy in loads:
        copy.start()
    for copy in loads:
        copy.wait()

    pl.semaphore_wait(barrier, chips + jnp.where(is_root, plane * chips, plane))

    swaps = [remote(v.rown.at[other_rows], v.rin, v.swap_s.at[0], v.swap_r.at[0], sibling)]
    for i in range(3):
        part = fac.at[i, core]
        swaps.append(remote(part, part, v.swap_s.at[i + 1], v.swap_r.at[i + 1], sibling))
    for copy in swaps:
        copy.start()

    @pl.when(is_root)
    def _():
        for g in range(groups - 1):
            @pl.when(plane > g)
            def _(g=g):
                for c in range(chips):
                    signal(v.up, (g, c * 2 + core))

    for copy in swaps[:3]:
        copy.wait_recv()
    mine = v.rown[mine_rows]
    theirs = v.rin[...]
    r_first = jnp.where(core == 0, mine, theirs)
    r_second = jnp.where(core == 0, theirs, mine)

    y_copy = remote(v.yout, v.yin, v.y_s, v.y_r, near(jnp.minimum(chip + 1, root)))
    yl_copy = remote(v.yout, v.yin, v.yl_s, v.y_r, near(last))
    o_copy = remote(v.yout, v.oin, v.o_s, v.o_r, near(last))
    u_copy = remote(v.uout, v.uin, v.u_s, v.u_r, near(jnp.minimum(chip + 1, root)))
    pair_to = near(jnp.where(is_last, root, last))
    e_copy = remote(v.maps.at[jnp.where(is_last, 1, 0), core], v.edge.at[core], v.e_s, v.e_r, pair_to)
    e_onward = remote(v.edge.at[core], v.edge.at[core], v.ef_s, v.ef_r, sibling)
    e_theirs = remote(v.edge.at[other], v.edge.at[other], v.ef_s, v.ef_r, sibling)
    at_edge = chip >= root
    below = root - 1
    g_copy = remote(v.maps.at[1, core], v.far.at[0, core], v.g_s, v.g_r.at[0], near(below))
    h_copy = remote(v.maps.at[1, core], v.far.at[1, core], v.g_s, v.g_r.at[1], near(below))
    d_copy = remote(v.tout2.at[core], v.tn.at[core], v.d_s, v.d_r, near(jnp.maximum(chip - 1, 0)))

    def across(buf, k, send, recv):
        return remote(buf.at[k], buf.at[k], send, recv, sibling)

    def d_across(k):
        return across(v.tn, k, v.df_s, v.df_r)

    def far_across(i, k):
        return across(v.far.at[i], k, v.gf_s.at[i], v.gf_r.at[i])

    u_copies = []
    for step in range(1, groups):
        g = lax.rem(plane + step, groups)
        u_copies.append(
            remote(v.uout, v.ubuf.at[0, plane], v.ux_s.at[step], v.ux_r.at[0, plane], (g, root * 2 + core))
        )
    ul_copies = []
    for step in reversed(range(groups)):
        g = lax.rem(plane + step, groups)
        ul_copies.append(
            remote(v.uout, v.ubuf.at[1, plane], v.ux_s.at[step], v.ux_r.at[1, plane], (g, root * 2 + core))
        )

    own_first = times_t(r_first, fac[0, 0])
    own_second = times_t(r_second - times_t(own_first, fac[1, 1]), fac[0, 1])

    @pl.when(chip == 0)
    def _():
        v.yin[...] = jnp.zeros_like(v.yin)
        v.yout[...] = own_second
        y_copy.start()
        if root == 1:
            yl_copy.start()

    @pl.when(is_root)
    def _():
        v.yout[...] = own_second
        o_copy.start()

    @pl.when(plane < groups - 1)
    def _():
        pl.semaphore_wait(v.up, groups - 1 - plane)

    def sep_copy(g):
        return remote(sp_ref, v.sep.at[core, chip, plane], v.sep_s.at[g], v.sep_r.at[chip], (g, root * 2 + core))

    useful = chip >= (plane * wide) // (2 * deep)

    def sep_away(action):
        for g in reversed(range(groups)):
            @pl.when(jnp.logical_and(useful, plane != g))
            def _(g=g):
                action(sep_copy(g))

    def sep_near(action):
        for g in range(groups):
            @pl.when(jnp.logical_and(jnp.logical_and(useful, plane == g), jnp.logical_not(is_root)))
            def _(g=g):
                action(sep_copy(g))

    def peers(action):
        for g in range(groups):
            @pl.when(plane != g)
            def _(g=g):
                action(g, (g, root * 2 + core))

    def rs_copy(g, to, at):
        return remote(rs_ref.at[mine_rows], v.rsbuf.at[at], v.rs_s.at[g], v.rs_r.at[at], to)

    def id_copy(g, to, at):
        return remote(idx_ref, v.idx.at[at], v.id_s.at[g], v.id_r.at[at], to)

    own_rs = pltpu.make_async_copy(rs_ref.at[mine_rows], v.rsbuf.at[plane], v.loc_s.at[4])
    own_id = pltpu.make_async_copy(idx_ref, v.idx.at[plane], v.loc_s.at[5])

    @pl.when(is_root)
    def _():
        own_rs.start()
        own_id.start()
        peers(lambda g, to: id_copy(g, to, plane).start())
        peers(lambda g, to: rs_copy(g, to, plane).start())

        @pl.when(useful)
        def _():
            pltpu.make_async_copy(sp_ref, v.sep.at[core, root, plane], v.sep_r.at[root]).start()

    sep_away(lambda copy: copy.start())

    swaps[3].wait_recv()
    own_update = times_t(own_first, fac[2, 0]) + times_t(own_second, fac[2, 1])

    @pl.when(chip == 0)
    def _():
        v.uout[...] = own_update
        u_copy.start()

    early = split(dot(fac[0, 0], fac[1, 0]))
    late = split(dot(fac[0, 1], fac[1, 1]))
    whole = split(composed(late, early))
    for part in range(2):
        v.maps[0, part] = whole[part]

    @pl.when(is_root)
    def _():
        e_copy.start()

    seen = split(
        dot(fac[2, 1], whole[0]) - dot(fac[2, 0], early[0])
        + (dot(fac[2, 1], whole[1]) - dot(fac[2, 0], early[1]))
    )
    for part in range(2):
        v.maps[1, part] = seen[part]

    @pl.when(is_last)
    def _():
        g_copy.start()

    upper, lower = pl.ds(0, fac.shape[2] // 2), pl.ds(fac.shape[2] // 2, fac.shape[2] // 2)
    quarters = ((upper, upper), (lower, pl.ds(0, fac.shape[2])))

    def map_copies(c, to):
        return [
            remote(
                v.maps.at[0, core, rows, columns], v.later.at[c - 1, 0, core, rows, columns],
                v.m_s.at[i, to], v.m_r.at[i, c - 1], near(to),
            )
            for i, (rows, columns) in enumerate(quarters)
        ]

    def map_start(c, to):
        for copy in map_copies(c, to):
            copy.start()

    def map_sent(c, to):
        for copy in map_copies(c, to):
            copy.wait_send()

    def map_onward(i, c, k):
        part = v.later.at[c - 1, i, k]
        return remote(part, part, v.mf_s.at[i, c - 1], v.mf_r.at[i, c - 1], sibling)

    def turned_copy(c, to):
        return remote(v.tout, v.tbuf.at[c - 1], v.t_s.at[to], v.t_r.at[c - 1], near(to))

    def to_earlier(places, action):
        for c in places:
            @pl.when(chip == c)
            def _(c=c):
                for to in reversed(range(c)):
                    action(c, to)

    def from_later(places, action):
        for c in places:
            @pl.when(chip < c)
            def _(c=c):
                action(c)

    to_earlier([root], map_start)

    @pl.when(is_root)
    def _():
        h_copy.start()

    sep_near(lambda copy: copy.start())

    @pl.when(is_last)
    def _():
        e_copy.start()

    @pl.when(is_root)
    def _():
        for g in range(groups):
            for c in range(skips[g]):
                v.sep[:, c, g] = jnp.zeros((2, deep, wide), BF16)
        own_id.wait()
        own_rs.wait()
        peers(lambda g, to: id_copy(g, to, g).wait_recv())
        lanes = min(128, picks)
        for g in range(groups):
            index = jnp.transpose(jnp.broadcast_to(v.idx[g].astype(F32), (lanes, picks)))
            for at in range(0, groups * wide, lanes):
                column = lax.broadcasted_iota(jnp.int32, (picks, lanes), 1) + at
                v.sel[g * picks : (g + 1) * picks, at : at + lanes] = (
                    (index == column.astype(F32)).astype(F32).astype(BF16)
                )

    def edge_arrives():
        e_copy.wait_recv()
        e_onward.start()
        e_theirs.wait_recv()

    @pl.when(is_last)
    def _():
        edge_arrives()

    @pl.when(chip > 0)
    def _():
        y_copy.wait_recv()

    @pl.when(is_last)
    def _():
        o_copy.wait_recv()
        v.yin[...] = v.oin[...] + through(v.yin[...], (v.edge[0], v.edge[1]), dot_t)

    heard = v.yin[...]
    second = own_second + through(heard, whole, dot_t)

    @pl.when(is_mid)
    def _():
        v.yout[...] = second
        y_copy.start()

        @pl.when(chip == root - 1)
        def _():
            yl_copy.start()

        update = own_update + through(heard, seen, dot_t)
        u_copy.wait_recv()
        v.uout[...] = update + v.uin[...]
        u_copy.start()

    @pl.when(at_edge)
    def _():
        v.uout[...] = own_update + through(heard, seen, dot_t)

    @pl.when(is_last)
    def _():
        for copy in ul_copies:
            copy.start()

    @pl.when(is_root)
    def _():
        u_copy.wait_recv()
        v.uout[...] += v.uin[...]
        for copy in u_copies:
            copy.start()

    to_earlier(range(1, root), map_start)
    first = own_first - times_t(times_t(heard, fac[1, 0]), fac[0, 0])
    v.tout[...] = times(times(first, fac[0, 0]), fac[1, 0]) - through(second, whole, dot)
    to_earlier(range(1, chips), lambda c, to: turned_copy(c, to).start())

    def final_maps():
        back = split(dot(fac[2, 1], fac[0, 1]) + dot(v.tn[0], fac[0, 1]) + dot(v.tn[1], fac[0, 1]))
        between = split(dot(back[0], fac[1, 1]) + dot(back[1], fac[1, 1]))
        ahead = split(dot(fac[2, 0], fac[0, 0]) - (dot(between[0], fac[0, 0]) + dot(between[1], fac[0, 0])))
        for part in range(2):
            v.fmap[0, part] = ahead[part]
            v.fmap[1, part] = back[part]

    x_copy = remote(v.xs.at[other], v.obuf.at[core], v.x_s, v.x_r, sibling)

    def step_back(c):
        turned_copy(c, 0).wait_recv()
        if c == last:
            v.vin[...] = v.tbuf[c - 1]
        else:
            v.vin[...] = v.tbuf[c - 1] + through(v.vin[...], (v.later[c - 1, 0, 0], v.later[c - 1, 0, 1]), dot)

    def plain_part():
        v.vin[...] = jnp.zeros_like(v.vin)
        from_later(reversed(range(1, chips)), step_back)
        k_second = times(second - v.vin[...], fac[0, 1])
        k_first = times(first - times(k_second, fac[1, 1]), fac[0, 0])
        v.xs[0] = k_first
        v.xs[1] = k_second
        v.obuf[core] = v.xs[core]
        x_copy.start()

    def block(g, c):
        return jnp.concatenate([v.sep[0, c, g], v.sep[1, c, g]], axis=0)

    def sep_part(c, k):
        return v.sep.at[k, c, pl.ds(0, sum(skip <= c for skip in skips))]

    def sep_onward(c, k):
        return remote(sep_part(c, k), sep_part(c, k), v.fwd_s.at[c], v.fwd_r.at[c], sibling)

    own_rows = pl.ds(pl.multiple_of(plane * picks, picks), picks)
    targets = [near(c) for c in reversed(range(root))] + [near(last)]
    z_copies = [remote(v.zbuf.at[core], v.zbuf.at[core], v.z_s.at[i], v.z_r.at[core], to) for i, to in enumerate(targets)]
    so_copies = [remote(v.sol.at[core], v.sol.at[core], v.so_s.at[i], v.so_r.at[core], to) for i, to in enumerate(targets)]
    z_across = remote(v.zbuf.at[core], v.zbuf.at[core], v.z_s.at[chips], v.z_r.at[core], sibling)
    so_across = remote(v.sol.at[core], v.sol.at[core], v.so_s.at[chips], v.so_r.at[core], sibling)

    @pl.when(is_root)
    def _():
        for c in range(chips):
            pltpu.make_async_copy(sep_part(c, core), sep_part(c, core), v.sep_r.at[c]).wait()
            sep_onward(c, core).start()
        peers(lambda g, to: rs_copy(g, to, g).wait_recv())

        for c in range(chips):
            sep_onward(c, other).wait_recv()
            taken = 0
            for g in range(groups):
                if skips[g] <= c:
                    taken = taken + dot_t(v.sel[own_rows, g * wide : (g + 1) * wide], block(g, c))
            v.at[c] = taken.astype(BF16)

        def from_last(g):
            remote(v.uout, v.ubuf.at[1, g], v.ux_s.at[0], v.ux_r.at[1, g], sibling).wait_recv()

        from_last(plane)
        total = times(v.uout[...] + v.ubuf[1, plane], v.sel[own_rows])
        for step in range(1, groups):
            g = lax.rem(plane + step, groups)
            remote(v.uout, v.ubuf.at[0, g], v.ux_s.at[step], v.ux_r.at[0, g], sibling).wait_recv()
            from_last(g)
            rows = pl.ds(pl.multiple_of(g * picks, picks), picks)
            total = total + times(v.ubuf[0, g] + v.ubuf[1, g], v.sel[rows])
        parts = [halves(v.rsbuf[g] - total[:, g * wide : (g + 1) * wide]) for g in range(groups)]
        found, ahead = 0, []
        for c in range(chips):
            value = 0
            for g in range(groups):
                if skips[g] <= c:
                    value = value + dot_t(parts[g], block(g, c))
            ahead.append(halves(joined(value)))
            found = found + dot_t(ahead[c], v.at[c])
        v.zbuf[core] = joined(found)
        for copy in z_copies:
            copy.start()
        z_across.start()
        solved = 0
        for c in range(chips):
            solved = solved + dot(ahead[c], block(plane, c))
        v.sol[core] = joined(solved)
        for copy in so_copies:
            copy.start()
        so_across.start()
        plain_part()
        edge_arrives()
        for part in range(2):
            v.tn[part] = v.edge[part]
        final_maps()

    def pass_on(i, c):
        for copy in map_copies(c, 0):
            copy.wait_recv()
        map_onward(i, c, core).start()

    def send_down():
        value = seen[0].astype(F32) + seen[1].astype(F32) + composed((v.tn[0], v.tn[1]), whole)
        for part, value in enumerate(split(value)):
            v.tout2[part] = value
        d_copy.start()

    @pl.when(jnp.logical_not(is_root))
    def _():
        @pl.when(chip == below)
        def _():
            g_copy.wait_recv()
            far_across(0, core).start()

        from_later(reversed(range(1, last)), functools.partial(pass_on, 0))

        @pl.when(chip == below)
        def _():
            h_copy.wait_recv()
            far_across(1, core).start()

        from_later(reversed(range(1, last)), lambda c: map_onward(0, c, other).wait_recv())

        @pl.when(chip == below)
        def _():
            far_across(0, other).wait_recv()
            far_across(1, other).wait_recv()
            value = v.far[1, 0].astype(F32) + v.far[1, 1].astype(F32) + composed(
                (v.far[0, 0], v.far[0, 1]), (v.later[root - 1, 0, 0], v.later[root - 1, 0, 1])
            )
            for part, value in enumerate(split(value)):
                v.tn[part] = value

            @pl.when(chip > 0)
            def _():
                send_down()

        plain_part()

        @pl.when(is_last)
        def _():
            v.tn[...] = jnp.zeros_like(v.tn)

        @pl.when(chip < below)
        def _():
            d_copy.wait_recv()
            d_across(core).start()
            d_across(other).wait_recv()

            @pl.when(chip > 0)
            def _():
                send_down()

        final_maps()

    x_copy.wait_recv()

    def solved_rows(k, rows):
        moved = through(v.zbuf[k], (v.fmap[core, 0], v.fmap[core, 1]), dot)
        out_ref[rows] = v.obuf[k] - moved

    @pl.when(jnp.logical_not(is_root))
    def _():
        z_copies[0].wait_recv()
        z_across.start()

    solved_rows(core, mine_rows)
    remote(v.zbuf.at[other], v.zbuf.at[other], v.z_s.at[chips], v.z_r.at[other], sibling).wait_recv()
    solved_rows(other, other_rows)

    @pl.when(jnp.logical_not(is_root))
    def _():
        so_copies[0].wait_recv()
        so_across.start()

    sol_ref[mine_rows] = v.sol[core]
    remote(v.sol.at[other], v.sol.at[other], v.so_s.at[chips], v.so_r.at[other], sibling).wait_recv()
    sol_ref[other_rows] = v.sol[other]

    for copy in swaps:
        copy.wait_send()
    sep_away(lambda copy: copy.wait_send())
    sep_near(lambda copy: copy.wait_send())

    @pl.when(chip < root)
    def _():
        y_copy.wait_send()
        u_copy.wait_send()

    @pl.when(chip == root - 1)
    def _():
        yl_copy.wait_send()

    @pl.when(at_edge)
    def _():
        e_copy.wait_send()
        e_onward.wait_send()

    @pl.when(is_last)
    def _():
        for copy in ul_copies:
            copy.wait_send()

    @pl.when(is_last)
    def _():
        g_copy.wait_send()

    @pl.when(is_root)
    def _():
        h_copy.wait_send()

    @pl.when(chip == below)
    def _():
        for i in range(2):
            far_across(i, core).wait_send()

    @pl.when(jnp.logical_and(chip > 0, chip < root))
    def _():
        d_copy.wait_send()

    @pl.when(chip < below)
    def _():
        d_across(core).wait_send()

    to_earlier(range(1, last), map_sent)
    from_later(range(1, last), lambda c: map_onward(0, c, core).wait_send())
    to_earlier(range(1, chips), lambda c, to: turned_copy(c, to).wait_send())

    @pl.when(is_root)
    def _():
        o_copy.wait_send()
        peers(lambda g, to: id_copy(g, to, plane).wait_send())
        peers(lambda g, to: rs_copy(g, to, plane).wait_send())
        for c in range(chips):
            sep_onward(c, core).wait_send()
        for copy in u_copies + z_copies + so_copies:
            copy.wait_send()

    x_copy.wait_send()
    z_across.wait_send()
    so_across.wait_send()


def store(x_ref, s_ref, out_ref, sol_ref, sems):
    copies = [
        pltpu.make_async_copy(x_ref, out_ref, sems.at[0]),
        pltpu.make_async_copy(s_ref, sol_ref, sems.at[1]),
    ]
    for copy in copies:
        copy.start()
    for copy in copies:
        copy.wait()


def solution(mesh):
    groups, fronts = mesh.shape["leaf"], mesh.shape["front"]
    chips = fronts // 2

    def shards(rhs_leaf, diag_inv, sub_block, coupling, update_rows, rhs_sep, sep_inv):
        width, columns = rhs_leaf.shape[1:]
        picks = coupling.shape[1]
        wide = rhs_sep.shape[0]
        deep = sep_inv.shape[0]
        half = columns // 2
        skips = tuple(g * wide // (2 * deep) for g in range(groups))
        vmem, dma = pltpu.VMEM, pltpu.SemaphoreType.DMA
        scratch = dict(
            fac=vmem((3, 2, width, width), BF16),
            rown=vmem((columns, width), F32),
            rin=vmem((half, width), F32),
            maps=vmem((2, 2, width, width), BF16),
            edge=vmem((2, width, width), BF16),
            later=vmem((chips - 2, 1, 2, width, width), BF16),
            far=vmem((2, 2, width, width), BF16),
            tout2=vmem((2, picks, width), BF16),
            tn=vmem((2, picks, width), BF16),
            fmap=vmem((2, 2, picks, width), BF16),
            tout=vmem((half, width), F32),
            tbuf=vmem((chips - 1, half, width), F32),
            yin=vmem((half, width), F32),
            yout=vmem((half, width), F32),
            oin=vmem((half, width), F32),
            uin=vmem((half, picks), F32),
            uout=vmem((half, picks), F32),
            ubuf=vmem((2, groups, half, picks), F32),
            rsbuf=vmem((groups, half, wide), F32),
            idx=vmem((groups, 1, picks), jnp.int32),
            sep=vmem((2, chips, groups, deep, wide), BF16),
            sel=vmem((groups * picks, groups * wide), BF16),
            at=vmem((chips, picks, 2 * deep), BF16),
            zbuf=vmem((2, half, picks), F32),
            sol=vmem((2, half, wide), F32),
            vin=vmem((half, width), F32),
            xs=vmem((2, half, width), F32),
            obuf=vmem((2, half, width), F32),
            up=pltpu.SemaphoreType.REGULAR,
            loc_s=dma((6,)), swap_s=dma((4,)), swap_r=dma((4,)),
            y_s=dma, y_r=dma, yl_s=dma, o_s=dma, o_r=dma, u_s=dma, u_r=dma,
            e_s=dma, e_r=dma, ef_s=dma, ef_r=dma,
            ux_s=dma((groups,)), ux_r=dma((2, groups)), rs_s=dma((groups,)), rs_r=dma((groups,)),
            id_s=dma((groups,)), id_r=dma((groups,)), sep_s=dma((groups,)), sep_r=dma((chips,)),
            fwd_s=dma((chips,)), fwd_r=dma((chips,)),
            m_s=dma((2, chips)), m_r=dma((2, chips)), mf_s=dma((1, chips)), mf_r=dma((1, chips)),
            g_s=dma, g_r=dma((2,)), gf_s=dma((2,)), gf_r=dma((2,)), d_s=dma, d_r=dma, df_s=dma, df_r=dma,
            t_s=dma((chips,)), t_r=dma((chips,)),
            z_s=dma((chips + 1,)), z_r=dma((2,)), so_s=dma((chips + 1,)), so_r=dma((2,)),
            x_s=dma, x_r=dma,
        )
        out, sol = pl.pallas_call(
            functools.partial(kernel, groups, chips, skips, tuple(scratch)),
            out_shape=(vmem((columns, width), F32), vmem((columns, wide), F32)),
            in_specs=[pl.BlockSpec(memory_space=pltpu.HBM)] * 7,
            out_specs=(pl.BlockSpec(memory_space=vmem), pl.BlockSpec(memory_space=vmem)),
            scratch_shapes=list(scratch.values()),
            compiler_params=pltpu.CompilerParams(
                collective_id=0, has_side_effects=True, vmem_limit_bytes=65344 * 1024
            ),
        )(
            rhs_leaf[0].T, diag_inv[0, 0], sub_block[0, 0], coupling[0],
            update_rows, rhs_sep.T, sep_inv,
        )
        hbm = pl.BlockSpec(memory_space=pltpu.HBM)
        out, sol = pl.pallas_call(
            store,
            out_shape=(
                jax.ShapeDtypeStruct((columns, width), F32),
                jax.ShapeDtypeStruct((columns, wide), F32),
            ),
            in_specs=[pl.BlockSpec(memory_space=vmem)] * 2,
            out_specs=(hbm, hbm),
            scratch_shapes=[dma((2,))],
            compiler_params=pltpu.CompilerParams(vmem_limit_bytes=1024 * 1024),
        )(out, sol)
        return out.T[None], sol.T

    return jax.shard_map(
        shards,
        mesh=mesh,
        in_specs=(
            P("leaf", "front", None),
            P("leaf", "front", None, None),
            P("leaf", "front", None, None),
            P("leaf", None, "front"),
            P("leaf", None),
            P("leaf", None),
            P("front", "leaf"),
        ),
        out_specs=(P("leaf", "front", None), P("leaf", None)),
        check_vma=False,
    )
```

```python
import functools
import types

import jax
import jax.numpy as jnp
from jax import lax
from jax.experimental import pallas as pl
from jax.experimental.pallas import tpu as pltpu
from jax.sharding import PartitionSpec as P

MESH = pl.DeviceIdType.MESH
F32 = jnp.float32
BF16 = jnp.bfloat16


def halves(x):
    head = x.astype(BF16)
    rest = (x - head.astype(F32)).astype(BF16)
    return jnp.concatenate([head, rest], axis=0)


def joined(both):
    rows = both.shape[0] // 2
    return both[:rows] + both[rows:]


def dot(a, b):
    return jnp.dot(a, b, preferred_element_type=F32)


def dot_t(a, b):
    return lax.dot_general(a, b, (((1,), (1,)), ((), ())), preferred_element_type=F32)


def times(x, w):
    return joined(dot(halves(x), w))


def times_t(x, w):
    return joined(dot_t(halves(x), w))


def split(x):
    head = x.astype(BF16)
    return head, (x - head.astype(F32)).astype(BF16)


def through(x, w, multiply):
    head, rest = w
    both = halves(x)
    return joined(multiply(both, head)) + multiply(both[: x.shape[0]], rest)


def composed(a, b):
    return dot(a[0], b[0]) + (dot(a[1], b[0]) + dot(a[0], b[1]))


def kernel(groups, chips, skips, names, r_ref, d_ref, b_ref, c_ref, idx_ref, rs_ref, sp_ref, out_ref, sol_ref, *refs):
    v = types.SimpleNamespace(**dict(zip(names, refs)))
    plane = lax.axis_index("leaf")
    front = lax.axis_index("front")
    chip = front // 2
    core = front % 2
    other = 1 - core
    last = chips - 1
    root = chips - 2
    is_root = chip == root
    is_last = chip == last
    is_mid = jnp.logical_and(chip > 0, chip < root)
    sibling = (plane, chip * 2 + other)
    half = v.yin.shape[0]
    picks = v.uin.shape[1]
    deep, wide = v.sep.shape[3:]
    fac = v.fac

    def remote(src, dst, send, recv, to):
        return pltpu.make_async_remote_copy(
            src_ref=src, dst_ref=dst, send_sem=send, recv_sem=recv, device_id=to, device_id_type=MESH
        )

    def near(c):
        return (plane, c * 2 + core)

    mine_rows = pl.ds(pl.multiple_of(core * half, half), half)
    other_rows = pl.ds(pl.multiple_of(other * half, half), half)

    barrier = pltpu.get_barrier_semaphore()

    def signal(sem, to):
        pl.semaphore_signal(sem, inc=1, device_id=to, device_id_type=MESH)

    signal(barrier, sibling)
    for c in range(chips):
        @pl.when(chip != c)
        def _(c=c):
            signal(barrier, near(c))
    for g in range(1, groups):
        @pl.when(plane < g)
        def _(g=g):
            @pl.when(is_root)
            def _():
                for c in range(chips):
                    signal(barrier, (g, c * 2 + core))

            @pl.when(jnp.logical_not(is_root))
            def _():
                signal(barrier, (g, root * 2 + core))

    @pl.when(chip < root)
    def _():
        edge_at = fac.shape[2] // 2
        for c in range(chips - 2):
            for k in range(2):
                v.later[c, 0, k, :edge_at, edge_at:] = jnp.zeros((edge_at, fac.shape[2] - edge_at), BF16)

    @pl.when(is_last)
    def _():
        edge_at = fac.shape[2] // 2
        for k in range(2):
            v.edge[k, :edge_at, edge_at:] = jnp.zeros((edge_at, fac.shape[2] - edge_at), BF16)

    loads = [pltpu.make_async_copy(r_ref, v.rown, v.loc_s.at[0])]
    for i, ref in enumerate((d_ref, b_ref, c_ref)):
        loads.append(pltpu.make_async_copy(ref, fac.at[i, core], v.loc_s.at[i + 1]))
    for copy in loads:
        copy.start()
    for copy in loads:
        copy.wait()

    pl.semaphore_wait(barrier, chips + jnp.where(is_root, plane * chips, plane))

    swaps = [remote(v.rown.at[other_rows], v.rin, v.swap_s.at[0], v.swap_r.at[0], sibling)]
    for i in range(3):
        part = fac.at[i, core]
        swaps.append(remote(part, part, v.swap_s.at[i + 1], v.swap_r.at[i + 1], sibling))
    for copy in swaps:
        copy.start()

    @pl.when(is_root)
    def _():
        for g in range(groups - 1):
            @pl.when(plane > g)
            def _(g=g):
                for c in range(chips):
                    signal(v.up, (g, c * 2 + core))

    for copy in swaps[:3]:
        copy.wait_recv()
    mine = v.rown[mine_rows]
    theirs = v.rin[...]
    r_first = jnp.where(core == 0, mine, theirs)
    r_second = jnp.where(core == 0, theirs, mine)

    y_copy = remote(v.yout, v.yin, v.y_s, v.y_r, near(jnp.minimum(chip + 1, root)))
    yl_copy = remote(v.yout, v.yin, v.yl_s, v.y_r, near(last))
    o_copy = remote(v.yout, v.oin, v.o_s, v.o_r, near(last))
    u_copy = remote(v.uout, v.uin, v.u_s, v.u_r, near(jnp.minimum(chip + 1, root)))
    e_copy = remote(v.maps.at[1, core], v.edge.at[core], v.e_s, v.e_r, near(root))
    upper, lower = pl.ds(0, fac.shape[2] // 2), pl.ds(fac.shape[2] // 2, fac.shape[2] // 2)
    quarters = ((upper, upper), (lower, pl.ds(0, fac.shape[2])))
    w_copies = [
        remote(
            v.maps.at[0, core, rows, columns], v.edge.at[core, rows, columns], v.w_s.at[i], v.w_r.at[i], near(last)
        )
        for i, (rows, columns) in enumerate(quarters)
    ]
    e_onward = remote(v.edge.at[core], v.edge.at[core], v.ef_s, v.ef_r, sibling)
    e_theirs = remote(v.edge.at[other], v.edge.at[other], v.ef_s, v.ef_r, sibling)
    at_edge = chip >= root
    below = root - 1
    g_copy = remote(v.maps.at[1, core], v.far.at[0, core], v.g_s, v.g_r.at[0], near(below))
    h_copy = remote(v.maps.at[1, core], v.far.at[1, core], v.g_s, v.g_r.at[1], near(below))
    d_copy = remote(v.tout2.at[core], v.tn.at[core], v.d_s, v.d_r, near(jnp.maximum(chip - 1, 0)))

    def across(buf, k, send, recv):
        return remote(buf.at[k], buf.at[k], send, recv, sibling)

    def d_across(k):
        return across(v.tn, k, v.df_s, v.df_r)

    def far_across(i, k):
        return across(v.far.at[i], k, v.gf_s.at[i], v.gf_r.at[i])

    u_copies = []
    for step in range(1, groups):
        g = lax.rem(plane + step, groups)
        u_copies.append(
            remote(v.uout, v.ubuf.at[0, plane], v.ux_s.at[step], v.ux_r.at[0, plane], (g, root * 2 + core))
        )
    ul_copies = []
    for step in reversed(range(groups)):
        g = lax.rem(plane + step, groups)
        ul_copies.append(
            remote(v.uout, v.ubuf.at[1, plane], v.ux_s.at[step], v.ux_r.at[1, plane], (g, root * 2 + core))
        )

    own_first = times_t(r_first, fac[0, 0])
    own_second = times_t(r_second - times_t(own_first, fac[1, 1]), fac[0, 1])

    @pl.when(chip == 0)
    def _():
        v.yin[...] = jnp.zeros_like(v.yin)
        v.yout[...] = own_second
        y_copy.start()
        if root == 1:
            yl_copy.start()

    @pl.when(is_root)
    def _():
        v.yout[...] = own_second
        o_copy.start()

    @pl.when(plane < groups - 1)
    def _():
        pl.semaphore_wait(v.up, groups - 1 - plane)

    def sep_copy(g):
        return remote(sp_ref, v.sep.at[core, chip, plane], v.sep_s.at[g], v.sep_r.at[chip], (g, root * 2 + core))

    useful = chip >= (plane * wide) // (2 * deep)

    def sep_away(action):
        for g in reversed(range(groups)):
            @pl.when(jnp.logical_and(useful, plane != g))
            def _(g=g):
                action(sep_copy(g))

    def sep_near(action):
        for g in range(groups):
            @pl.when(jnp.logical_and(jnp.logical_and(useful, plane == g), jnp.logical_not(is_root)))
            def _(g=g):
                action(sep_copy(g))

    def peers(action):
        for g in range(groups):
            @pl.when(plane != g)
            def _(g=g):
                action(g, (g, root * 2 + core))

    def rs_copy(g, to, at):
        return remote(rs_ref.at[mine_rows], v.rsbuf.at[at], v.rs_s.at[g], v.rs_r.at[at], to)

    def id_copy(g, to, at):
        return remote(idx_ref, v.idx.at[at], v.id_s.at[g], v.id_r.at[at], to)

    own_rs = pltpu.make_async_copy(rs_ref.at[mine_rows], v.rsbuf.at[plane], v.loc_s.at[4])
    own_id = pltpu.make_async_copy(idx_ref, v.idx.at[plane], v.loc_s.at[5])

    @pl.when(is_root)
    def _():
        own_rs.start()
        own_id.start()
        peers(lambda g, to: id_copy(g, to, plane).start())
        peers(lambda g, to: rs_copy(g, to, plane).start())

        @pl.when(useful)
        def _():
            pltpu.make_async_copy(sp_ref, v.sep.at[core, root, plane], v.sep_r.at[root]).start()

    sep_away(lambda copy: copy.start())

    swaps[3].wait_recv()
    own_update = times_t(own_first, fac[2, 0]) + times_t(own_second, fac[2, 1])

    @pl.when(chip == 0)
    def _():
        v.uout[...] = own_update
        u_copy.start()

    early = split(dot(fac[0, 0], fac[1, 0]))
    late = split(dot(fac[0, 1], fac[1, 1]))
    whole = split(composed(late, early))
    for part in range(2):
        v.maps[0, part] = whole[part]

    @pl.when(is_root)
    def _():
        for copy in w_copies:
            copy.start()

    seen = split(
        dot(fac[2, 1], whole[0]) - dot(fac[2, 0], early[0])
        + (dot(fac[2, 1], whole[1]) - dot(fac[2, 0], early[1]))
    )
    for part in range(2):
        v.maps[1, part] = seen[part]

    @pl.when(is_last)
    def _():
        g_copy.start()

    def map_copies(c, to):
        return [
            remote(
                v.maps.at[0, core, rows, columns], v.later.at[c - 1, 0, core, rows, columns],
                v.m_s.at[i, to], v.m_r.at[i, c - 1], near(to),
            )
            for i, (rows, columns) in enumerate(quarters)
        ]

    def map_start(c, to):
        for copy in map_copies(c, to):
            copy.start()

    def map_sent(c, to):
        for copy in map_copies(c, to):
            copy.wait_send()

    def map_onward(i, c, k):
        part = v.later.at[c - 1, i, k]
        return remote(part, part, v.mf_s.at[i, c - 1], v.mf_r.at[i, c - 1], sibling)

    def turned_copy(c, to):
        return remote(v.tout, v.tbuf.at[c - 1], v.t_s.at[to], v.t_r.at[c - 1], near(to))

    def to_earlier(places, action):
        for c in places:
            @pl.when(chip == c)
            def _(c=c):
                for to in reversed(range(c)):
                    action(c, to)

    def from_later(places, action):
        for c in places:
            @pl.when(chip < c)
            def _(c=c):
                action(c)

    @pl.when(is_root)
    def _():
        h_copy.start()

    to_earlier([root], map_start)

    sep_near(lambda copy: copy.start())

    @pl.when(is_last)
    def _():
        e_copy.start()

    @pl.when(is_root)
    def _():
        for g in range(groups):
            for c in range(skips[g]):
                v.sep[:, c, g] = jnp.zeros((2, deep, wide), BF16)
        own_id.wait()
        own_rs.wait()
        peers(lambda g, to: id_copy(g, to, g).wait_recv())
        lanes = min(128, picks)
        for g in range(groups):
            index = jnp.transpose(jnp.broadcast_to(v.idx[g].astype(F32), (lanes, picks)))
            for at in range(0, groups * wide, lanes):
                column = lax.broadcasted_iota(jnp.int32, (picks, lanes), 1) + at
                v.sel[g * picks : (g + 1) * picks, at : at + lanes] = (
                    (index == column.astype(F32)).astype(F32).astype(BF16)
                )

    def edge_arrives(copies):
        for copy in copies:
            copy.wait_recv()
        e_onward.start()
        e_theirs.wait_recv()

    @pl.when(is_last)
    def _():
        edge_arrives(w_copies)

    @pl.when(chip > 0)
    def _():
        y_copy.wait_recv()

    @pl.when(is_last)
    def _():
        o_copy.wait_recv()
        v.yin[...] = v.oin[...] + through(v.yin[...], (v.edge[0], v.edge[1]), dot_t)

    heard = v.yin[...]
    second = own_second + through(heard, whole, dot_t)

    @pl.when(is_mid)
    def _():
        v.yout[...] = second
        y_copy.start()

        @pl.when(chip == root - 1)
        def _():
            yl_copy.start()

        update = own_update + through(heard, seen, dot_t)
        u_copy.wait_recv()
        v.uout[...] = update + v.uin[...]
        u_copy.start()

    @pl.when(at_edge)
    def _():
        v.uout[...] = own_update + through(heard, seen, dot_t)

    @pl.when(is_last)
    def _():
        for copy in ul_copies:
            copy.start()

    @pl.when(is_root)
    def _():
        u_copy.wait_recv()
        v.uout[...] += v.uin[...]
        for copy in u_copies:
            copy.start()

    to_earlier(range(1, root), map_start)
    first = own_first - times_t(times_t(heard, fac[1, 0]), fac[0, 0])
    v.tout[...] = times(times(first, fac[0, 0]), fac[1, 0]) - through(second, whole, dot)
    to_earlier(range(1, chips), lambda c, to: turned_copy(c, to).start())

    def final_maps():
        back = split(dot(fac[2, 1], fac[0, 1]) + dot(v.tn[0], fac[0, 1]) + dot(v.tn[1], fac[0, 1]))
        between = split(dot(back[0], fac[1, 1]) + dot(back[1], fac[1, 1]))
        ahead = split(dot(fac[2, 0], fac[0, 0]) - (dot(between[0], fac[0, 0]) + dot(between[1], fac[0, 0])))
        for part in range(2):
            v.fmap[0, part] = ahead[part]
            v.fmap[1, part] = back[part]

    x_copy = remote(v.xs.at[other], v.obuf.at[core], v.x_s, v.x_r, sibling)

    def step_back(c):
        turned_copy(c, 0).wait_recv()
        if c == last:
            v.vin[...] = v.tbuf[c - 1]
        else:
            v.vin[...] = v.tbuf[c - 1] + through(v.vin[...], (v.later[c - 1, 0, 0], v.later[c - 1, 0, 1]), dot)

    def plain_part():
        v.vin[...] = jnp.zeros_like(v.vin)
        from_later(reversed(range(1, chips)), step_back)
        k_second = times(second - v.vin[...], fac[0, 1])
        k_first = times(first - times(k_second, fac[1, 1]), fac[0, 0])
        v.xs[0] = k_first
        v.xs[1] = k_second
        v.obuf[core] = v.xs[core]
        x_copy.start()

    def block(g, c):
        return jnp.concatenate([v.sep[0, c, g], v.sep[1, c, g]], axis=0)

    def sep_part(c, k):
        return v.sep.at[k, c, pl.ds(0, sum(skip <= c for skip in skips))]

    def sep_onward(c, k):
        return remote(sep_part(c, k), sep_part(c, k), v.fwd_s.at[c], v.fwd_r.at[c], sibling)

    own_rows = pl.ds(pl.multiple_of(plane * picks, picks), picks)
    targets = [near(c) for c in reversed(range(root))] + [near(last)]
    z_copies = [remote(v.zbuf.at[core], v.zbuf.at[core], v.z_s.at[i], v.z_r.at[core], to) for i, to in enumerate(targets)]
    so_copies = [remote(v.sol.at[core], v.sol.at[core], v.so_s.at[i], v.so_r.at[core], to) for i, to in enumerate(targets)]
    z_across = remote(v.zbuf.at[core], v.zbuf.at[core], v.z_s.at[chips], v.z_r.at[core], sibling)
    so_across = remote(v.sol.at[core], v.sol.at[core], v.so_s.at[chips], v.so_r.at[core], sibling)

    @pl.when(is_root)
    def _():
        for c in range(chips):
            pltpu.make_async_copy(sep_part(c, core), sep_part(c, core), v.sep_r.at[c]).wait()
            sep_onward(c, core).start()
        peers(lambda g, to: rs_copy(g, to, g).wait_recv())

        for c in range(chips):
            sep_onward(c, other).wait_recv()
            taken = 0
            for g in range(groups):
                if skips[g] <= c:
                    taken = taken + dot_t(v.sel[own_rows, g * wide : (g + 1) * wide], block(g, c))
            v.at[c] = taken.astype(BF16)

        def from_last(g):
            remote(v.uout, v.ubuf.at[1, g], v.ux_s.at[0], v.ux_r.at[1, g], sibling).wait_recv()

        from_last(plane)
        total = times(v.uout[...] + v.ubuf[1, plane], v.sel[own_rows])
        for step in range(1, groups):
            g = lax.rem(plane + step, groups)
            remote(v.uout, v.ubuf.at[0, g], v.ux_s.at[step], v.ux_r.at[0, g], sibling).wait_recv()
            from_last(g)
            rows = pl.ds(pl.multiple_of(g * picks, picks), picks)
            total = total + times(v.ubuf[0, g] + v.ubuf[1, g], v.sel[rows])
        parts = [halves(v.rsbuf[g] - total[:, g * wide : (g + 1) * wide]) for g in range(groups)]
        found, ahead = 0, []
        for c in range(chips):
            value = 0
            for g in range(groups):
                if skips[g] <= c:
                    value = value + dot_t(parts[g], block(g, c))
            ahead.append(halves(joined(value)))
            found = found + dot_t(ahead[c], v.at[c])
        v.zbuf[core] = joined(found)
        for copy in z_copies:
            copy.start()
        z_across.start()
        solved = 0
        for c in range(chips):
            solved = solved + dot(ahead[c], block(plane, c))
        v.sol[core] = joined(solved)
        for copy in so_copies:
            copy.start()
        so_across.start()
        plain_part()
        edge_arrives([e_copy])
        for part in range(2):
            v.tn[part] = v.edge[part]
        final_maps()

    def pass_on(i, c):
        for copy in map_copies(c, 0):
            copy.wait_recv()
        map_onward(i, c, core).start()

    def send_down():
        value = seen[0].astype(F32) + seen[1].astype(F32) + composed((v.tn[0], v.tn[1]), whole)
        for part, value in enumerate(split(value)):
            v.tout2[part] = value
        d_copy.start()

    @pl.when(jnp.logical_not(is_root))
    def _():
        @pl.when(chip == below)
        def _():
            g_copy.wait_recv()
            far_across(0, core).start()

        from_later(reversed(range(1, last)), functools.partial(pass_on, 0))

        @pl.when(chip == below)
        def _():
            h_copy.wait_recv()
            far_across(1, core).start()

        from_later(reversed(range(1, last)), lambda c: map_onward(0, c, other).wait_recv())

        @pl.when(chip == below)
        def _():
            far_across(0, other).wait_recv()
            far_across(1, other).wait_recv()
            value = v.far[1, 0].astype(F32) + v.far[1, 1].astype(F32) + composed(
                (v.far[0, 0], v.far[0, 1]), (v.later[root - 1, 0, 0], v.later[root - 1, 0, 1])
            )
            for part, value in enumerate(split(value)):
                v.tn[part] = value

            @pl.when(chip > 0)
            def _():
                send_down()

        plain_part()

        @pl.when(is_last)
        def _():
            v.tn[...] = jnp.zeros_like(v.tn)

        @pl.when(chip < below)
        def _():
            d_copy.wait_recv()
            d_across(core).start()
            d_across(other).wait_recv()

            @pl.when(chip > 0)
            def _():
                send_down()

        final_maps()

    x_copy.wait_recv()

    def solved_rows(k, rows):
        moved = through(v.zbuf[k], (v.fmap[core, 0], v.fmap[core, 1]), dot)
        out_ref[rows] = v.obuf[k] - moved

    @pl.when(jnp.logical_not(is_root))
    def _():
        z_copies[0].wait_recv()
        z_across.start()

    solved_rows(core, mine_rows)
    remote(v.zbuf.at[other], v.zbuf.at[other], v.z_s.at[chips], v.z_r.at[other], sibling).wait_recv()
    solved_rows(other, other_rows)

    @pl.when(jnp.logical_not(is_root))
    def _():
        so_copies[0].wait_recv()
        so_across.start()

    sol_ref[mine_rows] = v.sol[core]
    remote(v.sol.at[other], v.sol.at[other], v.so_s.at[chips], v.so_r.at[other], sibling).wait_recv()
    sol_ref[other_rows] = v.sol[other]

    for copy in swaps:
        copy.wait_send()
    sep_away(lambda copy: copy.wait_send())
    sep_near(lambda copy: copy.wait_send())

    @pl.when(chip < root)
    def _():
        y_copy.wait_send()
        u_copy.wait_send()

    @pl.when(chip == root - 1)
    def _():
        yl_copy.wait_send()

    @pl.when(at_edge)
    def _():
        e_onward.wait_send()

    @pl.when(is_last)
    def _():
        e_copy.wait_send()

    @pl.when(is_root)
    def _():
        for copy in w_copies:
            copy.wait_send()

    @pl.when(is_last)
    def _():
        for copy in ul_copies:
            copy.wait_send()

    @pl.when(is_last)
    def _():
        g_copy.wait_send()

    @pl.when(is_root)
    def _():
        h_copy.wait_send()

    @pl.when(chip == below)
    def _():
        for i in range(2):
            far_across(i, core).wait_send()

    @pl.when(jnp.logical_and(chip > 0, chip < root))
    def _():
        d_copy.wait_send()

    @pl.when(chip < below)
    def _():
        d_across(core).wait_send()

    to_earlier(range(1, last), map_sent)
    from_later(range(1, last), lambda c: map_onward(0, c, core).wait_send())
    to_earlier(range(1, chips), lambda c, to: turned_copy(c, to).wait_send())

    @pl.when(is_root)
    def _():
        o_copy.wait_send()
        peers(lambda g, to: id_copy(g, to, plane).wait_send())
        peers(lambda g, to: rs_copy(g, to, plane).wait_send())
        for c in range(chips):
            sep_onward(c, core).wait_send()
        for copy in u_copies + z_copies + so_copies:
            copy.wait_send()

    x_copy.wait_send()
    z_across.wait_send()
    so_across.wait_send()


def store(x_ref, s_ref, out_ref, sol_ref, sems):
    copies = [
        pltpu.make_async_copy(x_ref, out_ref, sems.at[0]),
        pltpu.make_async_copy(s_ref, sol_ref, sems.at[1]),
    ]
    for copy in copies:
        copy.start()
    for copy in copies:
        copy.wait()


def solution(mesh):
    groups, fronts = mesh.shape["leaf"], mesh.shape["front"]
    chips = fronts // 2

    def shards(rhs_leaf, diag_inv, sub_block, coupling, update_rows, rhs_sep, sep_inv):
        width, columns = rhs_leaf.shape[1:]
        picks = coupling.shape[1]
        wide = rhs_sep.shape[0]
        deep = sep_inv.shape[0]
        half = columns // 2
        skips = tuple(g * wide // (2 * deep) for g in range(groups))
        vmem, dma = pltpu.VMEM, pltpu.SemaphoreType.DMA
        scratch = dict(
            fac=vmem((3, 2, width, width), BF16),
            rown=vmem((columns, width), F32),
            rin=vmem((half, width), F32),
            maps=vmem((2, 2, width, width), BF16),
            edge=vmem((2, width, width), BF16),
            later=vmem((chips - 2, 1, 2, width, width), BF16),
            far=vmem((2, 2, width, width), BF16),
            tout2=vmem((2, picks, width), BF16),
            tn=vmem((2, picks, width), BF16),
            fmap=vmem((2, 2, picks, width), BF16),
            tout=vmem((half, width), F32),
            tbuf=vmem((chips - 1, half, width), F32),
            yin=vmem((half, width), F32),
            yout=vmem((half, width), F32),
            oin=vmem((half, width), F32),
            uin=vmem((half, picks), F32),
            uout=vmem((half, picks), F32),
            ubuf=vmem((2, groups, half, picks), F32),
            rsbuf=vmem((groups, half, wide), F32),
            idx=vmem((groups, 1, picks), jnp.int32),
            sep=vmem((2, chips, groups, deep, wide), BF16),
            sel=vmem((groups * picks, groups * wide), BF16),
            at=vmem((chips, picks, 2 * deep), BF16),
            zbuf=vmem((2, half, picks), F32),
            sol=vmem((2, half, wide), F32),
            vin=vmem((half, width), F32),
            xs=vmem((2, half, width), F32),
            obuf=vmem((2, half, width), F32),
            up=pltpu.SemaphoreType.REGULAR,
            loc_s=dma((6,)), swap_s=dma((4,)), swap_r=dma((4,)),
            y_s=dma, y_r=dma, yl_s=dma, o_s=dma, o_r=dma, u_s=dma, u_r=dma,
            e_s=dma, e_r=dma, w_s=dma((2,)), w_r=dma((2,)), ef_s=dma, ef_r=dma,
            ux_s=dma((groups,)), ux_r=dma((2, groups)), rs_s=dma((groups,)), rs_r=dma((groups,)),
            id_s=dma((groups,)), id_r=dma((groups,)), sep_s=dma((groups,)), sep_r=dma((chips,)),
            fwd_s=dma((chips,)), fwd_r=dma((chips,)),
            m_s=dma((2, chips)), m_r=dma((2, chips)), mf_s=dma((1, chips)), mf_r=dma((1, chips)),
            g_s=dma, g_r=dma((2,)), gf_s=dma((2,)), gf_r=dma((2,)), d_s=dma, d_r=dma, df_s=dma, df_r=dma,
            t_s=dma((chips,)), t_r=dma((chips,)),
            z_s=dma((chips + 1,)), z_r=dma((2,)), so_s=dma((chips + 1,)), so_r=dma((2,)),
            x_s=dma, x_r=dma,
        )
        out, sol = pl.pallas_call(
            functools.partial(kernel, groups, chips, skips, tuple(scratch)),
            out_shape=(vmem((columns, width), F32), vmem((columns, wide), F32)),
            in_specs=[pl.BlockSpec(memory_space=pltpu.HBM)] * 7,
            out_specs=(pl.BlockSpec(memory_space=vmem), pl.BlockSpec(memory_space=vmem)),
            scratch_shapes=list(scratch.values()),
            compiler_params=pltpu.CompilerParams(
                collective_id=0, has_side_effects=True, vmem_limit_bytes=65344 * 1024
            ),
        )(
            rhs_leaf[0].T, diag_inv[0, 0], sub_block[0, 0], coupling[0],
            update_rows, rhs_sep.T, sep_inv,
        )
        hbm = pl.BlockSpec(memory_space=pltpu.HBM)
        out, sol = pl.pallas_call(
            store,
            out_shape=(
                jax.ShapeDtypeStruct((columns, width), F32),
                jax.ShapeDtypeStruct((columns, wide), F32),
            ),
            in_specs=[pl.BlockSpec(memory_space=vmem)] * 2,
            out_specs=(hbm, hbm),
            scratch_shapes=[dma((2,))],
            compiler_params=pltpu.CompilerParams(vmem_limit_bytes=1024 * 1024),
        )(out, sol)
        return out.T[None], sol.T

    return jax.shard_map(
        shards,
        mesh=mesh,
        in_specs=(
            P("leaf", "front", None),
            P("leaf", "front", None, None),
            P("leaf", "front", None, None),
            P("leaf", None, "front"),
            P("leaf", None),
            P("leaf", None),
            P("front", "leaf"),
        ),
        out_specs=(P("leaf", "front", None), P("leaf", None)),
        check_vma=False,
    )
```
